256 devices in a mesh: gz: 128 (over x, y, z), gx: 2 (over core).
Axes of the slice: x: 4, y: 4, z: 8, core: 2. Of those that a mesh axis runs over, the one named last changes fastest.
Arguments:
- b_field: float32 [3, 48, 1024, 256], P(None, 'gx', 'gz'), may hold values from -6 to 6
- resist: float32 [48, 1024, 256], P('gx', 'gz'), may hold values from 0.05 to 0.8
- ymix: float32 [256, 256], replicated, may hold values from -0.5 to 1.5
- zmix: float32 [1024, 1024], replicated, may hold values from -0.5 to 1.5
Outputs:
- b_next: float32 [3, 48, 1024, 256], P(None, 'gx', 'gz')
- potential: float32 [3, 48, 1024, 256], P(None, 'gx', 'gz')
The draws below stay inside these ranges and needn't reach their ends.
All inputs are finite; a program needn't handle non-finite values.
Results may differ from the reference program's by a relative error of at most 0.000073.
Values sent between devices are 32-bit elements; how exact they have to be, the bound alone decides.
A program may use at most 64 MiB of HBM per device.

```python
import math
import jax
import jax.numpy as jnp
from jax import lax

NY = 256
NX = 48
NZ = 1024


def draw_ymix(key, part):
    noise = jax.random.normal(key, (NY, NY), jnp.float32)
    return jnp.eye(NY, dtype=jnp.float32) + 0.6 * noise * NY ** (-0.5)


def draw_zmix(key, part):
    subkey = jax.random.fold_in(key, 7)
    noise = jax.random.normal(subkey, (NZ, NZ), jnp.float32)
    return jnp.eye(NZ, dtype=jnp.float32) + 0.6 * noise * NZ ** (-0.5)


def block_levels(stream_key, extent, split, low, largest):
    level, own = 1.0, jax.random.fold_in(stream_key, 6)
    for dim, shards_of in split:
        heights = jnp.exp(jax.random.uniform(jax.random.fold_in(own, dim), (shards_of,), jnp.float32, low / len(split), largest / len(split)))
        level = level * jnp.repeat(heights, extent[dim] // shards_of).reshape([-1 if axis == dim else 1 for axis in range(len(extent))])
    return level


def centred(key, shape, width, reach, cuts=(), kind=jnp.bfloat16):
    result = width * jax.random.normal(key, shape, jnp.float32)
    if cuts:
        result = result * block_levels(key, shape, cuts, -0.22, 0.18)
    return jnp.clip(result, -reach, reach).astype(kind)


def setup_inputs(seed: int = 0) -> dict:
    key_list = jax.random.split(jax.random.key(seed), 5)
    return {
        "b_field": centred(key_list[0], (3, NX, NZ, NY), 1.0, 6.0, ((1, 2), (2, 128)), jnp.float32),
        "resist": jnp.clip(jnp.exp(math.log(0.8) - 2.7725887 * jax.random.uniform(key_list[1], (NX, NZ, NY), jnp.float32) ** block_levels(key_list[1], (NX, NZ, NY), ((0, 2), (1, 128)), -0.2, 0.2)), 0.05, 0.8),
        "ymix": draw_ymix(jax.random.fold_in(key_list[4], 71), 0),
        "zmix": draw_zmix(jax.random.fold_in(key_list[4], 71), 0),
    }


time_step = 0.1
friction = 1.0


def curl_of(padded):
    centre = padded[:, 1:-1, 1:-1, :]
    grad_x = (padded[:, 2:, 1:-1, :] - padded[:, :-2, 1:-1, :]) * 0.5
    grad_z = (padded[:, 1:-1, 2:, :] - padded[:, 1:-1, :-2, :]) * 0.5
    grad_y = (jnp.roll(centre, -1, 3) - jnp.roll(centre, 1, 3)) * 0.5
    return jnp.stack([grad_y[2] - grad_z[1], grad_z[0] - grad_x[2], grad_x[1] - grad_y[0]])


def cross_product(lhs_vec, rhs_vec):
    return jnp.stack([lhs_vec[1] * rhs_vec[2] - lhs_vec[2] * rhs_vec[1],
                      lhs_vec[2] * rhs_vec[0] - lhs_vec[0] * rhs_vec[2],
                      lhs_vec[0] * rhs_vec[1] - lhs_vec[1] * rhs_vec[0]])


def electric(current, field, resist):
    strength = jnp.sum(field * field, axis=0) + 1.0
    velocity = cross_product(current, field) / (friction * strength)
    return resist * current - cross_product(velocity, field)


def reference(b_field, resist, ymix, zmix):
    widths = ((0, 0), (1, 1), (1, 1), (0, 0))
    current = curl_of(jnp.pad(b_field, widths))
    efield = electric(current, b_field, resist)
    curl_e = curl_of(jnp.pad(efield, widths))
    stepped = b_field - time_step * curl_e
    along_y = jnp.einsum('cxzi,ij->cxzj', stepped, ymix, precision=lax.Precision.HIGHEST)
    b_next = jnp.einsum('cxmy,mk->cxky', along_y, zmix, precision=lax.Precision.HIGHEST)
    column = jnp.cumsum(b_next, axis=2) * (NZ ** -0.5)
    potential = jnp.stack([column[1], -column[0], column[2]])
    return b_next, potential
```

```python
import functools

import jax
import jax.numpy as jnp
from jax import lax
from jax.experimental import pallas as pl
from jax.experimental.pallas import tpu as pltpu
from jax.sharding import PartitionSpec as P

MESH = pl.DeviceIdType.MESH
F32, BF16 = jnp.float32, jnp.bfloat16
TIME_STEP = 0.1
NX, NZL, NY = 24, 8, 256
LINES = 3 * NX
SLABS = 128
XR = 32


def split(value):
    high = value.astype(BF16)
    return high, (value - high.astype(F32)).astype(BF16)


def dot(lhs, rhs, rhs_dim=0):
    return lax.dot_general(
        lhs, rhs, (((1,), (rhs_dim,)), ((), ())), preferred_element_type=F32
    )


def dot3(lhs, rhs, rhs_dim=0):
    (lhs_hi, lhs_lo), (rhs_hi, rhs_lo) = lhs, rhs
    small = dot(lhs_lo, rhs_hi, rhs_dim) + dot(lhs_hi, rhs_lo, rhs_dim)
    return small + dot(lhs_hi, rhs_hi, rhs_dim)


def diff(value, axis):
    size = value.shape[axis]
    return pltpu.roll(value, size - 1, axis) - pltpu.roll(value, 1, axis)


def halo_copies(b, res, bp, send, recv):
    gz, gx = lax.axis_index("gz"), lax.axis_index("gx")
    down, up = lax.rem(gz + SLABS - 1, SLABS), lax.rem(gz + 1, SLABS)
    other = 1 - gx
    near, far = (NX - 1) * other, gx + (NX - 2) * other
    near_row, far_row = 24 + 7 * other, 25 + 5 * other
    rows = slice(0, NX)
    same, cross = lambda z: {"gz": z}, lambda z: {"gz": z, "gx": other}
    plan = (
        (b.at[:, :, 0], bp.at[0:3, 10, rows], same(down)),
        (b.at[:, :, 7], bp.at[0:3, 1, rows], same(up)),
        (b.at[0:2, :, 1], bp.at[0:2, 11, rows], same(down)),
        (b.at[0:2, :, 6], bp.at[0:2, 0, rows], same(up)),
        (res.at[:, 0], bp.at[3, 10, rows], same(down)),
        (res.at[:, 7], bp.at[3, 1, rows], same(up)),
        (b.at[:, near], bp.at[0:3, 2:10, near_row], cross(gz)),
        (b.at[1:3, far], bp.at[1:3, 2:10, far_row], cross(gz)),
        (res.at[near], bp.at[3, 2:10, near_row], cross(gz)),
        (b.at[:, near, 0], bp.at[0:3, 10, near_row], cross(down)),
        (b.at[:, near, 7], bp.at[0:3, 1, near_row], cross(up)),
    )
    return [
        pltpu.make_async_remote_copy(
            src_ref=src,
            dst_ref=dst,
            send_sem=send.at[i],
            recv_sem=recv.at[i],
            device_id=where,
            device_id_type=MESH,
        )
        for i, (src, dst, where) in enumerate(plan)
    ]


def exchange(src, dst, send, recv, own):
    me = lax.axis_index("gz")
    pltpu.make_async_copy(src.at[:, me], dst.at[:, me], own).start()

    @pl.loop(1, SLABS)
    def _(step):
        peer = lax.rem(me + step, SLABS)
        pltpu.make_async_remote_copy(
            src_ref=src.at[:, peer],
            dst_ref=dst.at[:, me],
            send_sem=send,
            recv_sem=recv,
            device_id={"gz": peer},
            device_id_type=MESH,
        ).start()


def exchange_wait(src, dst, send, recv, own):
    rest = pl.ds(0, SLABS - 1)
    pltpu.make_async_copy(src.at[:, 0], dst.at[:, 0], own).wait()
    pltpu.make_async_copy(dst.at[:, rest], dst.at[:, rest], recv).wait()


def exchange_sent(src, send):
    rest = pl.ds(0, SLABS - 1)
    pltpu.make_async_copy(src.at[:, rest], src.at[:, rest], send).wait()


def electric_plane(bp, ef, p):
    bx, by, bz, rs = bp[0, p], bp[1, p], bp[2, p], bp[3, p]
    jx = (diff(bz, 1) - (bp[1, p + 1] - bp[1, p - 1])) * 0.5
    jy = ((bp[0, p + 1] - bp[0, p - 1]) - diff(bz, 0)) * 0.5
    jz = (diff(by, 0) - diff(bx, 1)) * 0.5
    square = bx * bx + by * by + bz * bz
    inverse = 1.0 / (square + 1.0)
    along = (jx * bx + jy * by + jz * bz) * inverse
    factor = rs + square * inverse
    ef[0, p - 1] = jx * factor - bx * along
    ef[1, p - 1] = jy * factor - by * along
    ef[2, p - 1] = jz * factor - bz * along


def stepped_plane(bp, ef, st, r):
    ex, ey, ez = ef[0, r + 1], ef[1, r + 1], ef[2, r + 1]
    half = 0.5 * TIME_STEP
    cx = diff(ez, 1) - (ef[1, r + 2] - ef[1, r])
    cy = (ef[0, r + 2] - ef[0, r]) - diff(ez, 0)
    cz = diff(ey, 0) - diff(ex, 1)
    for c, curl in enumerate((cx, cy, cz)):
        row = pl.multiple_of(LINES + r * LINES + c * NX, 8)
        st[pl.ds(row, NX), :] = (bp[c, r + 2] - half * curl)[0:NX]


def kernel(
    b, res, ymix, zmix, next_ref, pot_ref,
    bp, ef, st, yv, zv, zt, zhi, zlo, rhi, rlo, fsend, frecv, osend, orecv, o1, o2,
    hs, hr, s1, r1, s2, r2, own, loads,
):
    gz, gx = lax.axis_index("gz"), lax.axis_index("gx")
    load_b = [pltpu.make_async_copy(b.at[:, :, z], bp.at[0:3, z + 2, 0:NX], loads.at[0]) for z in range(NZL)]
    load_r = [pltpu.make_async_copy(res.at[:, z], bp.at[3, z + 2, 0:NX], loads.at[1]) for z in range(NZL)]
    load_y = pltpu.make_async_copy(ymix, yv, loads.at[2])
    load_z = [pltpu.make_async_copy(zmix.at[:, k * 128 : (k + 1) * 128], zv.at[k], loads.at[3]) for k in range(8)]
    for copy in (*load_b, *load_r, load_y, *load_z):
        copy.start()
    bp[:, :, NX:XR, :] = jnp.zeros((4, 12, XR - NX, NY), F32)

    barrier = pltpu.get_barrier_semaphore()
    other = 1 - gx
    down, up = lax.rem(gz + SLABS - 1, SLABS), lax.rem(gz + 1, SLABS)
    for z in (down, gz, up):
        pl.semaphore_signal(barrier, inc=1, device_id={"gz": z, "gx": other}, device_id_type=MESH)

    @pl.loop(1, SLABS)
    def _(step):
        peer = lax.rem(gz + step, SLABS)
        pl.semaphore_signal(barrier, inc=1, device_id={"gz": peer}, device_id_type=MESH)

    pl.semaphore_wait(barrier, SLABS + 2)
    halo = halo_copies(b, res, bp, hs, hr)
    for copy in halo:
        copy.start()

    st[0:LINES, :] = jnp.zeros((LINES, NY), F32)
    st[9 * LINES :, :] = jnp.zeros((st.shape[0] - 9 * LINES, NY), F32)
    load_y.wait()
    y_hi, y_lo = split(yv[...].T)
    pltpu.make_async_copy(bp.at[0:3, 2:10, 0:NX], bp.at[0:3, 2:10, 0:NX], loads.at[0]).wait()
    pltpu.make_async_copy(bp.at[3, 2:10, 0:NX], bp.at[3, 2:10, 0:NX], loads.at[1]).wait()
    for copy in halo:
        copy.wait()

    @pl.when(gz == 0)
    def _():
        bp[:, 0:2] = jnp.zeros((4, 2, XR, NY), F32)

    @pl.when(gz == SLABS - 1)
    def _():
        bp[:, 10:12] = jnp.zeros((4, 2, XR, NY), F32)

    @pl.loop(1, 11)
    def _(p):
        electric_plane(bp, ef, p)

    @pl.loop(0, NZL)
    def _(r):
        stepped_plane(bp, ef, st, r)

    lane = lax.broadcasted_iota(jnp.int32, (SLABS, 128), 1)
    below = None
    for q in range(NZL + 1):
        mixed = dot3((y_hi, y_lo), split(st[q * LINES : q * LINES + 128, :]), 1)
        if q:
            fsend[q - 1] = jnp.where(lane < LINES, mixed[0:128], below)
        below = mixed[128:256]
    ends = jnp.concatenate([st[r * LINES + 128 : r * LINES + 144, :] for r in range(NZL)], axis=0)
    fsend[NZL] = dot3((y_hi[128:256], y_lo[128:256]), split(ends), 1)
    exchange(fsend, frecv, s1, r1, own.at[0])

    pltpu.make_async_copy(zv, zv, loads.at[3]).wait()
    row_id = lax.broadcasted_iota(jnp.int32, (SLABS, SLABS), 0)
    col_id = lax.broadcasted_iota(jnp.int32, (SLABS, SLABS), 1)
    lower = (col_id < row_id).astype(F32)

    @pl.loop(0, NZL)
    def _(r):
        for k in range(8):
            zt[k * 128 : (k + 1) * 128, :] = zv[k, pl.ds(r, SLABS, stride=8), :].T
        column = pl.ds(pl.multiple_of(r * SLABS, SLABS), SLABS)
        total = jnp.zeros((SLABS, SLABS), F32)
        for k in range(8):
            part = zt[pl.ds(k, SLABS, stride=8), :]
            total = total + part
            zhi[k * 128 : (k + 1) * 128, column], zlo[k * 128 : (k + 1) * 128, column] = split(part)
        under = lax.dot_general(
            lower, total, (((1,), (0,)), ((), ())),
            precision=lax.Precision.HIGHEST, preferred_element_type=F32,
        )
        zhi[1024:1152, column], zlo[1024:1152, column] = split(under)

    exchange_wait(fsend, frecv, s1, r1, own.at[0])
    tail = frecv[NZL]
    for r in range(NZL):
        rows = slice(r * SLABS, (r + 1) * SLABS)
        rhi[rows, 0:128], rlo[rows, 0:128] = split(frecv[r])
        moved = pltpu.roll(tail, (128 - 16 * r) % 128, 1) if r else tail
        rhi[rows, 128:256], rlo[rows, 128:256] = split(moved)

    packed = jnp.zeros((SLABS, 128), F32)
    for k in range(9):
        rows = slice(k * SLABS, (k + 1) * SLABS)
        mixed = dot3((zhi[rows, :], zlo[rows, :]), (rhi[...], rlo[...]))
        osend[k] = mixed[:, 0:128]
        end = mixed[:, 128:256]
        if k < 8:
            moved = pltpu.roll(end, 16 * k, 1) if k else end
            packed = jnp.where((lane >= 16 * k) & (lane < 16 * k + 16), moved, packed)
        else:
            osend[10] = end
    osend[9] = packed
    exchange(osend, orecv, s2, r2, own.at[1])
    exchange_sent(fsend, s1)
    exchange_wait(osend, orecv, s2, r2, own.at[1])

    scale = float(NZL * SLABS) ** -0.5
    column = orecv[8].T
    end_column = orecv[10].T[0:16]
    ends = orecv[9].T
    pieces = (
        (0, 24, 0, 192, -1.0, 0), (24, 48, 192, 0, 1.0, 0), (48, 72, 384, 384, 1.0, 0),
        (72, 96, 0, 192, -1.0, 1), (96, 120, 192, 0, 1.0, 1), (120, 128, 384, 384, 1.0, 1),
    )
    for k in range(NZL):
        lines = orecv[k].T
        column = column + lines
        for first, last, at, to, sign, half in pieces:
            o1[half, pl.ds(at + k, last - first, stride=8), :] = lines[first:last]
            o2[half, pl.ds(to + k, last - first, stride=8), :] = column[first:last] * (sign * scale)
        end = ends[16 * k : 16 * k + 16]
        end_column = end_column + end
        o1[1, pl.ds(448 + k, 16, stride=8), :] = end
        o2[1, pl.ds(448 + k, 16, stride=8), :] = end_column * scale
    out = [
        pltpu.make_async_copy(src.at[half], dst.at[:, half * 128 : half * 128 + 128], loads.at[4 + 2 * i + half])
        for i, (src, dst) in enumerate(((o1, next_ref), (o2, pot_ref)))
        for half in range(2)
    ]
    for copy in out:
        copy.start()
    exchange_sent(osend, s2)
    for copy in out:
        copy.wait()


def on_device(b_field, resist, ymix, zmix):
    flat = (3 * NX * NZL, NY)
    dma = pltpu.SemaphoreType.DMA
    b_next, potential = pl.pallas_call(
        kernel,
        name="step",
        out_shape=(jax.ShapeDtypeStruct(flat, F32), jax.ShapeDtypeStruct(flat, F32)),
        in_specs=[pl.BlockSpec(memory_space=pl.ANY)] * 4,
        out_specs=[pl.BlockSpec(memory_space=pl.ANY)] * 2,
        scratch_shapes=[
            pltpu.VMEM((4, NZL + 4, XR, NY), F32),
            pltpu.VMEM((3, NZL + 2, XR, NY), F32),
            pltpu.VMEM((LINES * 10, NY), F32),
            pltpu.VMEM((NY, NY), F32),
            pltpu.VMEM((8, 1024, 128), F32),
            pltpu.VMEM((1024, 128), F32),
            pltpu.VMEM((1152, 1024), BF16),
            pltpu.VMEM((1152, 1024), BF16),
            pltpu.VMEM((1024, 256), BF16),
            pltpu.VMEM((1024, 256), BF16),
            pltpu.VMEM((9, SLABS, 128), F32),
            pltpu.VMEM((9, SLABS, 128), F32),
            pltpu.VMEM((11, SLABS, 128), F32),
            pltpu.VMEM((11, SLABS, 128), F32),
            pltpu.VMEM((2, flat[0], 128), F32),
            pltpu.VMEM((2, flat[0], 128), F32),
            dma((11,)), dma((11,)), dma(()), dma(()), dma(()), dma(()), dma((2,)), dma((8,)),
        ],
        compiler_params=pltpu.CompilerParams(
            collective_id=0, has_side_effects=True, vmem_limit_bytes=50 * 2**20
        ),
    )(b_field, resist, ymix, zmix)
    return b_next.reshape(b_field.shape), potential.reshape(b_field.shape)


def solution(mesh):
    in_specs = (P(None, "gx", "gz", None), P("gx", "gz", None), P(), P())
    out_specs = (P(None, "gx", "gz", None), P(None, "gx", "gz", None))
    return jax.shard_map(
        on_device, mesh=mesh, in_specs=in_specs, out_specs=out_specs, check_vma=False
    )
```

```python
import functools

import jax
import jax.numpy as jnp
from jax import lax
from jax.experimental import pallas as pl
from jax.experimental.pallas import tpu as pltpu
from jax.sharding import PartitionSpec as P

MESH = pl.DeviceIdType.MESH
F32, BF16 = jnp.float32, jnp.bfloat16
TIME_STEP = 0.1
NX, NZL, NY = 24, 8, 256
LINES = 3 * NX
SLABS = 128
XR = 32


def split(value):
    high = value.astype(BF16)
    return high, (value - high.astype(F32)).astype(BF16)


def dot(lhs, rhs, rhs_dim=0):
    return lax.dot_general(
        lhs, rhs, (((1,), (rhs_dim,)), ((), ())), preferred_element_type=F32
    )


def dot3(lhs, rhs, rhs_dim=0):
    (lhs_hi, lhs_lo), (rhs_hi, rhs_lo) = lhs, rhs
    small = dot(lhs_lo, rhs_hi, rhs_dim) + dot(lhs_hi, rhs_lo, rhs_dim)
    return small + dot(lhs_hi, rhs_hi, rhs_dim)


def diff(value, axis):
    size = value.shape[axis]
    return pltpu.roll(value, size - 1, axis) - pltpu.roll(value, 1, axis)


def halo_copies(b, res, bp, send, recv):
    gz, gx = lax.axis_index("gz"), lax.axis_index("gx")
    down, up = lax.rem(gz + SLABS - 1, SLABS), lax.rem(gz + 1, SLABS)
    other = 1 - gx
    near, far = (NX - 1) * other, gx + (NX - 2) * other
    near_row, far_row = 24 + 7 * other, 25 + 5 * other
    rows = slice(0, NX)
    same, cross = lambda z: {"gz": z}, lambda z: {"gz": z, "gx": other}
    plan = (
        (b.at[:, near], bp.at[0:3, 2:10, near_row], cross(gz)),
        (b.at[1:3, far], bp.at[1:3, 2:10, far_row], cross(gz)),
        (res.at[near], bp.at[3, 2:10, near_row], cross(gz)),
        (b.at[:, :, 0], bp.at[0:3, 10, rows], same(down)),
        (b.at[:, :, 7], bp.at[0:3, 1, rows], same(up)),
        (b.at[0:2, :, 1], bp.at[0:2, 11, rows], same(down)),
        (b.at[0:2, :, 6], bp.at[0:2, 0, rows], same(up)),
        (res.at[:, 0], bp.at[3, 10, rows], same(down)),
        (res.at[:, 7], bp.at[3, 1, rows], same(up)),
        (b.at[:, near, 0], bp.at[0:3, 10, near_row], cross(down)),
        (b.at[:, near, 7], bp.at[0:3, 1, near_row], cross(up)),
    )
    return [
        pltpu.make_async_remote_copy(
            src_ref=src,
            dst_ref=dst,
            send_sem=send.at[i],
            recv_sem=recv.at[i],
            device_id=where,
            device_id_type=MESH,
        )
        for i, (src, dst, where) in enumerate(plan)
    ]


def exchange(src, dst, first, last, send, recv, own):
    me = lax.axis_index("gz")
    if src.ndim == 2:
        part, every = lambda ref, d: ref.at[d], lambda ref: ref.at[0 : SLABS - 1]
    else:
        part, every = lambda ref, d: ref.at[first:last, d], lambda ref: ref.at[first:last, 0 : SLABS - 1]
    here = pltpu.make_async_copy(part(src, me), part(dst, me), own)
    here.start()

    @pl.loop(1, SLABS)
    def _(step):
        peer = lax.rem(me + step, SLABS)
        pltpu.make_async_remote_copy(
            src_ref=part(src, peer),
            dst_ref=part(dst, me),
            send_sem=send,
            recv_sem=recv,
            device_id={"gz": peer},
            device_id_type=MESH,
        ).start()

    def arrived():
        here.wait()
        pltpu.make_async_copy(every(dst), every(dst), recv).wait()

    def sent():
        pltpu.make_async_copy(every(src), every(src), send).wait()

    return arrived, sent


def electric_plane(bp, ef, p):
    bx, by, bz, rs = bp[0, p], bp[1, p], bp[2, p], bp[3, p]
    jx = (diff(bz, 1) - (bp[1, p + 1] - bp[1, p - 1])) * 0.5
    jy = ((bp[0, p + 1] - bp[0, p - 1]) - diff(bz, 0)) * 0.5
    jz = (diff(by, 0) - diff(bx, 1)) * 0.5
    square = bx * bx + by * by + bz * bz
    inverse = 1.0 / (square + 1.0)
    along = (jx * bx + jy * by + jz * bz) * inverse
    factor = rs + square * inverse
    ef[0, p - 1] = jx * factor - bx * along
    ef[1, p - 1] = jy * factor - by * along
    ef[2, p - 1] = jz * factor - bz * along


def stepped_plane(bp, ef, st, r):
    ex, ey, ez = ef[0, r + 1], ef[1, r + 1], ef[2, r + 1]
    half = 0.5 * TIME_STEP
    cx = diff(ez, 1) - (ef[1, r + 2] - ef[1, r])
    cy = (ef[0, r + 2] - ef[0, r]) - diff(ez, 0)
    cz = diff(ey, 0) - diff(ex, 1)
    for c, curl in enumerate((cx, cy, cz)):
        row = pl.multiple_of(LINES + r * LINES + c * NX, 8)
        st[pl.ds(row, NX), :] = (bp[c, r + 2] - half * curl)[0:NX]


def mix_rows(st, rows, mixer, out, tails, first, half):
    lane = lax.broadcasted_iota(jnp.int32, (SLABS, 128), 1)
    high, low = mixer
    blocks = {}
    for q in sorted({*rows, *(r + 1 for r in rows)}):
        blocks[q] = dot3(mixer, split(st[q * LINES : q * LINES + 128, :]), 1)
    for i, r in enumerate(rows):
        out[first + i] = jnp.where(lane < LINES, blocks[r + 1][0:128], blocks[r][128:256])
    ends = jnp.concatenate([st[r * LINES + 128 : r * LINES + 144, :] for r in rows], axis=0)
    tails[half] = dot3((high[128:256], low[128:256]), split(ends), 1)


def prepare(zv, zt, zhi, zlo, first, last):
    row_id = lax.broadcasted_iota(jnp.int32, (SLABS, SLABS), 0)
    col_id = lax.broadcasted_iota(jnp.int32, (SLABS, SLABS), 1)
    lower = (col_id < row_id).astype(F32)

    @pl.loop(first, last)
    def _(slot):
        r = lax.rem(slot + 2, NZL)
        for k in range(8):
            zt[k * 128 : (k + 1) * 128, :] = zv[k, pl.ds(r, SLABS, stride=8), :].T
        column = pl.ds(pl.multiple_of(slot * SLABS, SLABS), SLABS)
        total = jnp.zeros((SLABS, SLABS), F32)
        for k in range(8):
            part = zt[pl.ds(k, SLABS, stride=8), :]
            total = total + part
            zhi[k * 128 : (k + 1) * 128, column], zlo[k * 128 : (k + 1) * 128, column] = split(part)
        under = lax.dot_general(
            lower, total, (((1,), (0,)), ((), ())),
            precision=lax.Precision.HIGHEST, preferred_element_type=F32,
        )
        zhi[1024:1152, column], zlo[1024:1152, column] = split(under)


def take_rows(frecv, trecv, rhi, rlo, half):
    zeros = jnp.zeros((SLABS, 64), F32)
    tail = jnp.concatenate([trecv[half], zeros], axis=1)
    for i in range(4):
        slot = 4 * half + i
        rows = slice(slot * SLABS, (slot + 1) * SLABS)
        rhi[rows, 0:128], rlo[rows, 0:128] = split(frecv[slot])
        moved = pltpu.roll(tail, 128 - 16 * i, 1) if i else tail
        rhi[rows, 128:256], rlo[rows, 128:256] = split(moved)


def kernel(
    b, res, ymix, zmix, next_ref, pot_ref,
    bp, ef, st, yv, zv, zt, zhi, zlo, rhi, rlo, acc,
    fsend, frecv, tsend, trecv, osend, orecv, esend, erecv, o1, o2,
    hs, hr, send, recv, own, loads,
):
    gz, gx = lax.axis_index("gz"), lax.axis_index("gx")
    load_b = [pltpu.make_async_copy(b.at[:, :, z], bp.at[0:3, z + 2, 0:NX], loads.at[0]) for z in range(NZL)]
    load_r = [pltpu.make_async_copy(res.at[:, z], bp.at[3, z + 2, 0:NX], loads.at[1]) for z in range(NZL)]
    load_y = pltpu.make_async_copy(ymix, yv, loads.at[2])
    load_z = [pltpu.make_async_copy(zmix.at[:, k * 128 : (k + 1) * 128], zv.at[k], loads.at[3]) for k in range(8)]
    for copy in (*load_b, *load_r, load_y, *load_z):
        copy.start()
    bp[:, :, NX:XR, :] = jnp.zeros((4, 12, XR - NX, NY), F32)

    barrier = pltpu.get_barrier_semaphore()
    other = 1 - gx
    down, up = lax.rem(gz + SLABS - 1, SLABS), lax.rem(gz + 1, SLABS)
    for z in (down, gz, up):
        pl.semaphore_signal(barrier, inc=1, device_id={"gz": z, "gx": other}, device_id_type=MESH)

    @pl.loop(1, SLABS)
    def _(step):
        peer = lax.rem(gz + step, SLABS)
        pl.semaphore_signal(barrier, inc=1, device_id={"gz": peer}, device_id_type=MESH)

    st[...] = jnp.zeros(st.shape, F32)
    load_y.wait()
    mixer = split(yv[...].T)
    pl.semaphore_wait(barrier, SLABS + 2)
    halo = halo_copies(b, res, bp, hs, hr)
    for copy in halo:
        copy.start()

    pltpu.make_async_copy(bp.at[0:3, 2:10, 0:NX], bp.at[0:3, 2:10, 0:NX], loads.at[0]).wait()
    pltpu.make_async_copy(bp.at[3, 2:10, 0:NX], bp.at[3, 2:10, 0:NX], loads.at[1]).wait()
    for copy in halo[:3]:
        copy.wait()

    @pl.loop(3, 9)
    def _(p):
        electric_plane(bp, ef, p)

    @pl.loop(2, 6)
    def _(r):
        stepped_plane(bp, ef, st, r)

    mix_rows(st, (2, 3, 4, 5), mixer, fsend, tsend, 0, 0)
    waits = [
        exchange(fsend, frecv, 0, 4, send.at[0], recv.at[0], own.at[0]),
        exchange(tsend, trecv, 0, 1, send.at[1], recv.at[1], own.at[1]),
    ]
    for copy in halo[3:]:
        copy.wait()

    @pl.when(gz == 0)
    def _():
        bp[:, 0:2] = jnp.zeros((4, 2, XR, NY), F32)

    @pl.when(gz == SLABS - 1)
    def _():
        bp[:, 10:12] = jnp.zeros((4, 2, XR, NY), F32)

    for p in (1, 2, 9, 10):
        electric_plane(bp, ef, p)
    for r in (0, 1, 6, 7):
        stepped_plane(bp, ef, st, r)
    mix_rows(st, (6, 7, 0, 1), mixer, fsend, tsend, 4, 1)
    waits += [
        exchange(fsend, frecv, 4, 8, send.at[2], recv.at[2], own.at[2]),
        exchange(tsend, trecv, 1, 2, send.at[3], recv.at[3], own.at[3]),
    ]
    pltpu.make_async_copy(zv, zv, loads.at[3]).wait()
    prepare(zv, zt, zhi, zlo, 0, NZL)

    waits[0][0]()
    waits[1][0]()
    take_rows(frecv, trecv, rhi, rlo, 0)
    for k in range(9):
        rows = slice(k * SLABS, (k + 1) * SLABS)
        acc[rows, :] = dot3((zhi[rows, 0:512], zlo[rows, 0:512]), (rhi[0:512, :], rlo[0:512, :]))
    waits[2][0]()
    waits[3][0]()
    take_rows(frecv, trecv, rhi, rlo, 1)

    lane = lax.broadcasted_iota(jnp.int32, (SLABS, 128), 1)
    packed = jnp.zeros((SLABS, 128), F32)
    groups = ((0, 3), (3, 6), (6, 10))
    for g, (first, last) in enumerate(groups):
        for slot in range(first, min(last, 9)):
            k = (slot + 8) % 9
            rows = slice(k * SLABS, (k + 1) * SLABS)
            mixed = acc[rows, :] + dot3(
                (zhi[rows, 512:1024], zlo[rows, 512:1024]), (rhi[512:1024, :], rlo[512:1024, :])
            )
            osend[slot] = mixed[:, 0:128]
            end = mixed[:, 128:256]
            if slot:
                moved = pltpu.roll(end, 16 * k, 1) if k else end
                packed = jnp.where((lane >= 16 * k) & (lane < 16 * k + 16), moved, packed)
            else:
                esend[...] = end[:, 0:16]
        if g == 2:
            osend[9] = packed
        waits.append(exchange(osend, orecv, first, last, send.at[4 + g], recv.at[4 + g], own.at[4 + g]))
        if g == 0:
            waits.append(exchange(esend, erecv, 0, 0, send.at[7], recv.at[7], own.at[7]))
    for _, sent in waits[:4]:
        sent()

    scale = float(NZL * SLABS) ** -0.5
    pieces = (
        (0, 24, 0, 192, -1.0, 0), (24, 48, 192, 0, 1.0, 0), (48, 72, 384, 384, 1.0, 0),
        (72, 96, 0, 192, -1.0, 1), (96, 120, 192, 0, 1.0, 1), (120, 128, 384, 384, 1.0, 1),
    )
    column = None
    for (first, last), wait in zip(groups, (4, 6, 7)):
        waits[wait][0]()
        for slot in range(first, min(last, 9)):
            lines = orecv[slot].T
            if slot == 0:
                column = lines
                continue
            k = slot - 1
            column = column + lines
            for low, high, at, to, sign, half in pieces:
                o1[half, pl.ds(at + k, high - low, stride=8), :] = lines[low:high]
                o2[half, pl.ds(to + k, high - low, stride=8), :] = column[low:high] * (sign * scale)
    waits[5][0]()
    ends = orecv[9].T
    end_column = erecv[...].T
    for k in range(NZL):
        end = ends[16 * k : 16 * k + 16]
        end_column = end_column + end
        o1[1, pl.ds(448 + k, 16, stride=8), :] = end
        o2[1, pl.ds(448 + k, 16, stride=8), :] = end_column * scale
    out = [
        pltpu.make_async_copy(src.at[half], dst.at[:, half * 128 : half * 128 + 128], loads.at[4 + 2 * i + half])
        for i, (src, dst) in enumerate(((o1, next_ref), (o2, pot_ref)))
        for half in range(2)
    ]
    for copy in out:
        copy.start()
    for _, sent in waits[4:]:
        sent()
    for copy in out:
        copy.wait()


def on_device(b_field, resist, ymix, zmix):
    flat = (3 * NX * NZL, NY)
    dma = pltpu.SemaphoreType.DMA
    b_next, potential = pl.pallas_call(
        kernel,
        name="step",
        out_shape=(jax.ShapeDtypeStruct(flat, F32), jax.ShapeDtypeStruct(flat, F32)),
        in_specs=[pl.BlockSpec(memory_space=pl.ANY)] * 4,
        out_specs=[pl.BlockSpec(memory_space=pl.ANY)] * 2,
        scratch_shapes=[
            pltpu.VMEM((4, NZL + 4, XR, NY), F32),
            pltpu.VMEM((3, NZL + 2, XR, NY), F32),
            pltpu.VMEM((LINES * 10, NY), F32),
            pltpu.VMEM((NY, NY), F32),
            pltpu.VMEM((8, 1024, 128), F32),
            pltpu.VMEM((1024, 128), F32),
            pltpu.VMEM((1152, 1024), BF16),
            pltpu.VMEM((1152, 1024), BF16),
            pltpu.VMEM((1024, 256), BF16),
            pltpu.VMEM((1024, 256), BF16),
            pltpu.VMEM((1152, 256), F32),
            pltpu.VMEM((8, SLABS, 128), F32),
            pltpu.VMEM((8, SLABS, 128), F32),
            pltpu.VMEM((2, SLABS, 64), F32),
            pltpu.VMEM((2, SLABS, 64), F32),
            pltpu.VMEM((10, SLABS, 128), F32),
            pltpu.VMEM((10, SLABS, 128), F32),
            pltpu.VMEM((SLABS, 16), F32),
            pltpu.VMEM((SLABS, 16), F32),
            pltpu.VMEM((2, flat[0], 128), F32),
            pltpu.VMEM((2, flat[0], 128), F32),
            dma((11,)), dma((11,)), dma((8,)), dma((8,)), dma((8,)), dma((8,)),
        ],
        compiler_params=pltpu.CompilerParams(
            collective_id=0, has_side_effects=True, vmem_limit_bytes=63 * 2**20
        ),
    )(b_field, resist, ymix, zmix)
    return b_next.reshape(b_field.shape), potential.reshape(b_field.shape)


def solution(mesh):
    in_specs = (P(None, "gx", "gz", None), P("gx", "gz", None), P(), P())
    out_specs = (P(None, "gx", "gz", None), P(None, "gx", "gz", None))
    return jax.shard_map(
        on_device, mesh=mesh, in_specs=in_specs, out_specs=out_specs, check_vma=False
    )
```

```python
import functools

import jax
import jax.numpy as jnp
from jax import lax
from jax.experimental import pallas as pl
from jax.experimental.pallas import tpu as pltpu
from jax.sharding import PartitionSpec as P

MESH = pl.DeviceIdType.MESH
F32, BF16 = jnp.float32, jnp.bfloat16
TIME_STEP = 0.1
NX, NZL, NY = 24, 8, 256
LINES = 3 * NX
SLABS = 128
XR = 32


def split(value):
    high = value.astype(BF16)
    return high, (value - high.astype(F32)).astype(BF16)


def dot(lhs, rhs, rhs_dim=0):
    return lax.dot_general(
        lhs, rhs, (((1,), (rhs_dim,)), ((), ())), preferred_element_type=F32
    )


def dot3(lhs, rhs, rhs_dim=0):
    (lhs_hi, lhs_lo), (rhs_hi, rhs_lo) = lhs, rhs
    small = dot(lhs_lo, rhs_hi, rhs_dim) + dot(lhs_hi, rhs_lo, rhs_dim)
    return small + dot(lhs_hi, rhs_hi, rhs_dim)


def diff(value, axis):
    size = value.shape[axis]
    return pltpu.roll(value, size - 1, axis) - pltpu.roll(value, 1, axis)


def halo_copies(b, res, bp, send, recv):
    gz, gx = lax.axis_index("gz"), lax.axis_index("gx")
    down, up = lax.rem(gz + SLABS - 1, SLABS), lax.rem(gz + 1, SLABS)
    other = 1 - gx
    near, far = (NX - 1) * other, gx + (NX - 2) * other
    near_row, far_row = 24 + 7 * other, 25 + 5 * other
    rows = slice(0, NX)
    same, cross = lambda z: {"gz": z}, lambda z: {"gz": z, "gx": other}
    plan = (
        (b.at[:, near], bp.at[0:3, 2:10, near_row], cross(gz)),
        (b.at[1:3, far], bp.at[1:3, 2:10, far_row], cross(gz)),
        (res.at[near], bp.at[3, 2:10, near_row], cross(gz)),
        (b.at[:, :, 0], bp.at[0:3, 10, rows], same(down)),
        (b.at[:, :, 7], bp.at[0:3, 1, rows], same(up)),
        (b.at[0:2, :, 1], bp.at[0:2, 11, rows], same(down)),
        (b.at[0:2, :, 6], bp.at[0:2, 0, rows], same(up)),
        (res.at[:, 0], bp.at[3, 10, rows], same(down)),
        (res.at[:, 7], bp.at[3, 1, rows], same(up)),
        (b.at[:, near, 0], bp.at[0:3, 10, near_row], cross(down)),
        (b.at[:, near, 7], bp.at[0:3, 1, near_row], cross(up)),
    )
    return [
        pltpu.make_async_remote_copy(
            src_ref=src,
            dst_ref=dst,
            send_sem=send.at[i],
            recv_sem=recv.at[i],
            device_id=where,
            device_id_type=MESH,
        )
        for i, (src, dst, where) in enumerate(plan)
    ]


def exchange(src, dst, spare, send, recv):
    me = lax.axis_index("gz")
    pltpu.make_async_copy(src.at[me], dst.at[me], recv).start()
    pltpu.make_async_copy(src.at[me], spare.at[0], send).start()

    @pl.loop(1, SLABS)
    def _(step):
        peer = lax.rem(me + step, SLABS)
        pltpu.make_async_remote_copy(
            src_ref=src.at[peer],
            dst_ref=dst.at[me],
            send_sem=send,
            recv_sem=recv,
            device_id={"gz": peer},
            device_id_type=MESH,
        ).start()

    def arrived():
        pltpu.make_async_copy(dst, dst, recv).wait()

    def sent():
        pltpu.make_async_copy(src, src, send).wait()

    return arrived, sent


def electric_plane(bp, ef, p):
    bx, by, bz, rs = bp[0, p], bp[1, p], bp[2, p], bp[3, p]
    jx = (diff(bz, 1) - (bp[1, p + 1] - bp[1, p - 1])) * 0.5
    jy = ((bp[0, p + 1] - bp[0, p - 1]) - diff(bz, 0)) * 0.5
    jz = (diff(by, 0) - diff(bx, 1)) * 0.5
    square = bx * bx + by * by + bz * bz
    inverse = 1.0 / (square + 1.0)
    along = (jx * bx + jy * by + jz * bz) * inverse
    factor = rs + square * inverse
    ef[0, p - 1] = jx * factor - bx * along
    ef[1, p - 1] = jy * factor - by * along
    ef[2, p - 1] = jz * factor - bz * along


def stepped_plane(bp, ef, st, r):
    ex, ey, ez = ef[0, r + 1], ef[1, r + 1], ef[2, r + 1]
    half = 0.5 * TIME_STEP
    cx = diff(ez, 1) - (ef[1, r + 2] - ef[1, r])
    cy = (ef[0, r + 2] - ef[0, r]) - diff(ez, 0)
    cz = diff(ey, 0) - diff(ex, 1)
    for c, curl in enumerate((cx, cy, cz)):
        row = pl.multiple_of(r * LINES + c * NX, 8)
        st[pl.ds(row, NX), :] = (bp[c, r + 2] - half * curl)[0:NX]


def mix_rows(rows, mixer, out, half):
    mixed = dot3(mixer, split(rows), 1)
    out[half] = mixed[0:SLABS]
    out[2 + half] = mixed[SLABS:]


def prepare(zv, zt, zhi, zlo, first, last):
    row_id = lax.broadcasted_iota(jnp.int32, (SLABS, SLABS), 0)
    col_id = lax.broadcasted_iota(jnp.int32, (SLABS, SLABS), 1)
    lower = (col_id < row_id).astype(F32)

    @pl.loop(first, last)
    def _(slot):
        r = lax.rem(slot + 2, NZL)
        for k in range(8):
            zt[k * 128 : (k + 1) * 128, :] = zv[k, pl.ds(r, SLABS, stride=8), :].T
        column = pl.ds(pl.multiple_of(slot * SLABS, SLABS), SLABS)
        total = jnp.zeros((SLABS, SLABS), F32)
        for k in range(8):
            part = zt[pl.ds(k, SLABS, stride=8), :]
            total = total + part
            zhi[k * 128 : (k + 1) * 128, column], zlo[k * 128 : (k + 1) * 128, column] = split(part)
        under = lax.dot_general(
            lower, total, (((1,), (0,)), ((), ())),
            precision=lax.Precision.HIGHEST, preferred_element_type=F32,
        )
        zhi[1024:1152, column], zlo[1024:1152, column] = split(under)


def take_rows(frecv, rhi, rlo, stream, half):
    lane = lax.broadcasted_iota(jnp.int32, (SLABS, 128), 1)
    got = frecv[2 * stream + half]
    got = jnp.concatenate([got, jnp.zeros((SLABS, 96), F32)], axis=1)
    for i in range(4):
        tile, off = divmod(i * LINES, 128)
        lines = got[:, tile * 128 : tile * 128 + 128]
        if off:
            lines = pltpu.roll(lines, 128 - off, 1)
        if off + LINES > 128:
            more = got[:, tile * 128 + 128 : tile * 128 + 256]
            lines = jnp.where(lane < 128 - off, lines, pltpu.roll(more, 128 - off, 1))
        row = (4 * half + i) * SLABS
        rhi[stream, row : row + SLABS, :], rlo[stream, row : row + SLABS, :] = split(lines)


def pack(pieces):
    lane = lax.broadcasted_iota(jnp.int32, (SLABS, 128), 1)
    tiles = {}
    for at, block in pieces:
        tile, off = divmod(at, 128)
        moved = pltpu.roll(block, off, 1) if off else block
        tiles[tile] = jnp.where(lane >= off, moved, tiles[tile]) if off else moved
        if off + LINES > 128:
            tiles[tile + 1] = moved
    return tiles


def mix_lines(zhi, zlo, rhi, rlo, osend, below, stream):
    pieces = []
    for first in range(0, 9, 3):
        rows = slice(first * SLABS, (first + 3) * SLABS)
        mixed = dot3((zhi[rows, :], zlo[rows, :]), (rhi[stream], rlo[stream]))
        for k in range(3):
            pieces.append(((first + k) * LINES, mixed[k * SLABS : (k + 1) * SLABS]))
    if stream == 0:
        below[...] = pieces.pop()[1]
    else:
        pieces[8:] = [(8 * LINES, below[...]), (9 * LINES, pieces[8][1])]
    for tile, value in pack(pieces).items():
        last = min(tile * 128 + 128, osend.shape[1])
        osend[:, tile * 128 : last] = value[:, 0 : last - tile * 128]


def kernel(
    b, res, ymix, zmix, ret0, ret1,
    bp, ef, st, yv, zv, zt, zhi, zlo, rhi, rlo, fsend, frecv, osend0, osend1, below,
    fspare, spare0, spare1, hs, hr, send, recv, loads,
):
    gz, gx = lax.axis_index("gz"), lax.axis_index("gx")
    load_b = [pltpu.make_async_copy(b.at[:, :, z], bp.at[0:3, z + 2, 0:NX], loads.at[0]) for z in range(NZL)]
    load_r = [pltpu.make_async_copy(res.at[:, z], bp.at[3, z + 2, 0:NX], loads.at[1]) for z in range(NZL)]
    load_y = pltpu.make_async_copy(ymix, yv, loads.at[2])
    load_z = [pltpu.make_async_copy(zmix.at[:, k * 128 : (k + 1) * 128], zv.at[k], loads.at[3]) for k in range(8)]
    for copy in (*load_b, *load_r, load_y, *load_z):
        copy.start()
    bp[:, :, NX:XR, :] = jnp.zeros((4, 12, XR - NX, NY), F32)

    barrier = pltpu.get_barrier_semaphore()
    other = 1 - gx
    down, up = lax.rem(gz + SLABS - 1, SLABS), lax.rem(gz + 1, SLABS)
    for z in (down, gz, up):
        pl.semaphore_signal(barrier, inc=1, device_id={"gz": z, "gx": other}, device_id_type=MESH)

    @pl.loop(1, SLABS)
    def _(step):
        peer = lax.rem(gz + step, SLABS)
        pl.semaphore_signal(barrier, inc=1, device_id={"gz": peer}, device_id_type=MESH)

    load_y.wait()
    mixer = split(yv[...].T)
    pl.semaphore_wait(barrier, SLABS + 2)
    halo = halo_copies(b, res, bp, hs, hr)
    for copy in halo:
        copy.start()

    pltpu.make_async_copy(bp.at[0:3, 2:10, 0:NX], bp.at[0:3, 2:10, 0:NX], loads.at[0]).wait()
    pltpu.make_async_copy(bp.at[3, 2:10, 0:NX], bp.at[3, 2:10, 0:NX], loads.at[1]).wait()
    for copy in halo[:3]:
        copy.wait()

    @pl.loop(3, 9)
    def _(p):
        electric_plane(bp, ef, p)

    @pl.loop(2, 6)
    def _(r):
        stepped_plane(bp, ef, st, r)

    mix_rows(st[2 * LINES : 6 * LINES, :], mixer, fsend, 0)
    waits = [exchange(fsend.at[0], frecv.at[0], fspare.at[0], send.at[0], recv.at[0])]
    for copy in halo[3:]:
        copy.wait()

    @pl.when(gz == 0)
    def _():
        bp[:, 0:2] = jnp.zeros((4, 2, XR, NY), F32)

    @pl.when(gz == SLABS - 1)
    def _():
        bp[:, 10:12] = jnp.zeros((4, 2, XR, NY), F32)

    for p in (1, 2, 9, 10):
        electric_plane(bp, ef, p)
    for r in (0, 1, 6, 7):
        stepped_plane(bp, ef, st, r)
    edges = jnp.concatenate([st[6 * LINES :, :], st[0 : 2 * LINES, :]], axis=0)
    mix_rows(edges, mixer, fsend, 1)
    for block in range(1, 4):
        waits.append(exchange(fsend.at[block], frecv.at[block], fspare.at[block], send.at[block], recv.at[block]))
    pltpu.make_async_copy(zv, zv, loads.at[3]).wait()
    prepare(zv, zt, zhi, zlo, 0, NZL)

    for stream, (osend, back, spare) in enumerate(((osend0, ret0, spare0), (osend1, ret1, spare1))):
        for half in range(2):
            waits[2 * stream + half][0]()
            take_rows(frecv, rhi, rlo, stream, half)
        mix_lines(zhi, zlo, rhi, rlo, osend, below, stream)
        waits.append(exchange(osend, back, spare, send.at[4 + stream], recv.at[4 + stream]))
    for _, sent in waits[:4]:
        sent()
    for arrived, sent in waits[4:]:
        arrived()
        sent()


def finish(ret0, ret1, next_ref, pot_ref, r0, r1, tv, o1, o2, loads):
    load = [pltpu.make_async_copy(ret0, r0, loads.at[0]), pltpu.make_async_copy(ret1, r1, loads.at[1])]
    for copy in load:
        copy.start()
    for stream, (copy, got) in enumerate(zip(load, (r0, r1))):
        copy.wait()
        width = got.shape[1]
        for at in range(0, width, 128):
            last = min(at + 128, width)
            tv[stream, at:last, :] = got[:, at:last].T

    scale = float(NZL * SLABS) ** -0.5
    out = []
    for stream in range(2):
        column = tv[1, (8 + stream) * LINES : (9 + stream) * LINES, :]
        for k in range(NZL):
            lines = tv[stream, k * LINES : (k + 1) * LINES, :]
            column = column + lines
            o1[stream, pl.ds(k, LINES, stride=8), :] = lines
            for at, to, sign in ((0, 192, -1.0), (24, 0, 1.0), (48, 384, 1.0)):
                o2[stream, pl.ds(to + k, NX, stride=8), :] = column[at : at + NX] * (sign * scale)
        for i, (src, dst) in enumerate(((o1, next_ref), (o2, pot_ref))):
            lanes = slice(stream * 128, stream * 128 + 128)
            out.append(pltpu.make_async_copy(src.at[stream], dst.at[:, lanes], loads.at[2 + 2 * stream + i]))
            out[-1].start()
    for copy in out:
        copy.wait()


def on_device(b_field, resist, ymix, zmix):
    flat = (3 * NX * NZL, NY)
    dma = pltpu.SemaphoreType.DMA
    anywhere = pl.BlockSpec(memory_space=pl.ANY)
    widths = (8 * LINES, 10 * LINES)
    returned = pl.pallas_call(
        kernel,
        name="step",
        out_shape=tuple(jax.ShapeDtypeStruct((SLABS, width), F32) for width in widths),
        in_specs=[anywhere] * 4,
        out_specs=[anywhere] * 2,
        scratch_shapes=[
            pltpu.VMEM((4, NZL + 4, XR, NY), F32),
            pltpu.VMEM((3, NZL + 2, XR, NY), F32),
            pltpu.VMEM((LINES * NZL, NY), F32),
            pltpu.VMEM((NY, NY), F32),
            pltpu.VMEM((8, 1024, 128), F32),
            pltpu.VMEM((1024, 128), F32),
            pltpu.VMEM((1152, 1024), BF16),
            pltpu.VMEM((1152, 1024), BF16),
            pltpu.VMEM((2, 1024, 128), BF16),
            pltpu.VMEM((2, 1024, 128), BF16),
            pltpu.VMEM((4, SLABS, 4 * LINES), F32),
            pltpu.VMEM((4, SLABS, 4 * LINES), F32),
            pltpu.VMEM((SLABS, widths[0]), F32),
            pltpu.VMEM((SLABS, widths[1]), F32),
            pltpu.VMEM((SLABS, 128), F32),
            pltpu.VMEM((4, 8, 4 * LINES), F32),
            pltpu.VMEM((8, widths[0]), F32),
            pltpu.VMEM((8, widths[1]), F32),
            dma((11,)), dma((11,)), dma((6,)), dma((6,)), dma((4,)),
        ],
        compiler_params=pltpu.CompilerParams(
            collective_id=0, has_side_effects=True, vmem_limit_bytes=63 * 2**20
        ),
    )(b_field, resist, ymix, zmix)
    b_next, potential = pl.pallas_call(
        finish,
        name="finish",
        out_shape=(jax.ShapeDtypeStruct(flat, F32), jax.ShapeDtypeStruct(flat, F32)),
        in_specs=[anywhere] * 2,
        out_specs=[anywhere] * 2,
        scratch_shapes=[
            pltpu.VMEM((SLABS, widths[0]), F32),
            pltpu.VMEM((SLABS, widths[1]), F32),
            pltpu.VMEM((2, widths[1], 128), F32),
            pltpu.VMEM((2, flat[0], 128), F32),
            pltpu.VMEM((2, flat[0], 128), F32),
            dma((6,)),
        ],
        compiler_params=pltpu.CompilerParams(vmem_limit_bytes=63 * 2**20),
    )(*returned)
    return b_next.reshape(b_field.shape), potential.reshape(b_field.shape)


def solution(mesh):
    in_specs = (P(None, "gx", "gz", None), P("gx", "gz", None), P(), P())
    out_specs = (P(None, "gx", "gz", None), P(None, "gx", "gz", None))
    return jax.shard_map(
        on_device, mesh=mesh, in_specs=in_specs, out_specs=out_specs, check_vma=False
    )
```

```python
import functools

import jax
import jax.numpy as jnp
from jax import lax
from jax.experimental import pallas as pl
from jax.experimental.pallas import tpu as pltpu
from jax.sharding import PartitionSpec as P

MESH = pl.DeviceIdType.MESH
F32, BF16 = jnp.float32, jnp.bfloat16
TIME_STEP = 0.1
NX, NZL, NY = 24, 8, 256
LINES = 3 * NX
SLABS = 128
XR = 32


def split(value):
    high = value.astype(BF16)
    return high, (value - high.astype(F32)).astype(BF16)


def dot(lhs, rhs, rhs_dim=0):
    return lax.dot_general(
        lhs, rhs, (((1,), (rhs_dim,)), ((), ())), preferred_element_type=F32
    )


def dot3(lhs, rhs, rhs_dim=0):
    (lhs_hi, lhs_lo), (rhs_hi, rhs_lo) = lhs, rhs
    small = dot(lhs_lo, rhs_hi, rhs_dim) + dot(lhs_hi, rhs_lo, rhs_dim)
    return small + dot(lhs_hi, rhs_hi, rhs_dim)


def diff(value, axis):
    size = value.shape[axis]
    return pltpu.roll(value, size - 1, axis) - pltpu.roll(value, 1, axis)


def halo_copies(bp, send, recv):
    gz, gx = lax.axis_index("gz"), lax.axis_index("gx")
    down, up = lax.rem(gz + SLABS - 1, SLABS), lax.rem(gz + 1, SLABS)
    other = 1 - gx
    near, far = (NX - 1) * other, gx + (NX - 2) * other
    near_row, far_row = 24 + 7 * other, 25 + 5 * other
    rows = slice(0, NX)
    same, cross = lambda z: {"gz": z}, lambda z: {"gz": z, "gx": other}
    plan = (
        (bp.at[:, 2:10, near], bp.at[:, 2:10, near_row], cross(gz)),
        (bp.at[1:3, 2:10, far], bp.at[1:3, 2:10, far_row], cross(gz)),
        (bp.at[:, 2, rows], bp.at[:, 10, rows], same(down)),
        (bp.at[:, 9, rows], bp.at[:, 1, rows], same(up)),
        (bp.at[0:3, 2, near], bp.at[0:3, 10, near_row], cross(down)),
        (bp.at[0:3, 9, near], bp.at[0:3, 1, near_row], cross(up)),
        (bp.at[0:2, 3, rows], bp.at[0:2, 11, rows], same(down)),
        (bp.at[0:2, 8, rows], bp.at[0:2, 0, rows], same(up)),
    )
    return [
        pltpu.make_async_remote_copy(
            src_ref=src,
            dst_ref=dst,
            send_sem=send.at[i],
            recv_sem=recv.at[i],
            device_id=where,
            device_id_type=MESH,
        )
        for i, (src, dst, where) in enumerate(plan)
    ]


def each_peer(me, act):
    for offsets in ((4,), (3, 5), (2, 6), (1, 7)):

        @pl.loop(0, 16)
        def _(step):
            row = me + 8 * lax.rem(10 + 5 * step, 16)
            for z in offsets:
                act(lax.rem(row + z, SLABS))

    @pl.loop(1, 16)
    def _(step):
        act(lax.rem(me + 8 * step, SLABS))


def exchange(src, dst, spare, send, recv):
    me = lax.axis_index("gz")
    pltpu.make_async_copy(src.at[me], dst.at[me], recv).start()
    pltpu.make_async_copy(src.at[me], spare.at[0], send).start()

    def push(peer):
        pltpu.make_async_remote_copy(
            src_ref=src.at[peer],
            dst_ref=dst.at[me],
            send_sem=send,
            recv_sem=recv,
            device_id={"gz": peer},
            device_id_type=MESH,
        ).start()

    each_peer(me, push)

    def arrived():
        pltpu.make_async_copy(dst, dst, recv).wait()

    def sent():
        pltpu.make_async_copy(src, src, send).wait()

    return arrived, sent


def electric_plane(bp, ef, p):
    bx, by, bz, rs = bp[0, p], bp[1, p], bp[2, p], bp[3, p]
    jx = (diff(bz, 1) - (bp[1, p + 1] - bp[1, p - 1])) * 0.5
    jy = ((bp[0, p + 1] - bp[0, p - 1]) - diff(bz, 0)) * 0.5
    jz = (diff(by, 0) - diff(bx, 1)) * 0.5
    square = bx * bx + by * by + bz * bz
    inverse = 1.0 / (square + 1.0)
    along = (jx * bx + jy * by + jz * bz) * inverse
    factor = rs + square * inverse
    ef[0, p - 1] = jx * factor - bx * along
    ef[1, p - 1] = jy * factor - by * along
    ef[2, p - 1] = jz * factor - bz * along


def stepped_plane(bp, ef, st, r):
    ex, ey, ez = ef[0, r + 1], ef[1, r + 1], ef[2, r + 1]
    half = 0.5 * TIME_STEP
    cx = diff(ez, 1) - (ef[1, r + 2] - ef[1, r])
    cy = (ef[0, r + 2] - ef[0, r]) - diff(ez, 0)
    cz = diff(ey, 0) - diff(ex, 1)
    for c, curl in enumerate((cx, cy, cz)):
        row = pl.multiple_of(r * LINES + c * NX, 8)
        st[pl.ds(row, NX), :] = (bp[c, r + 2] - half * curl)[0:NX]


def mix_rows(rows, mixer, out, half):
    mixed = dot3(mixer, split(rows), 1)
    out[half] = mixed[0:SLABS]
    out[2 + half] = mixed[SLABS:]


def prepare(zv, zt, zhi, zlo, first, last):
    row_id = lax.broadcasted_iota(jnp.int32, (SLABS, SLABS), 0)
    col_id = lax.broadcasted_iota(jnp.int32, (SLABS, SLABS), 1)
    lower = (col_id < row_id).astype(F32)

    @pl.loop(first, last)
    def _(slot):
        r = lax.rem(slot + 2, NZL)
        for k in range(8):
            zt[k * 128 : (k + 1) * 128, :] = zv[k, pl.ds(r, SLABS, stride=8), :].T
        column = pl.ds(pl.multiple_of(slot * SLABS, SLABS), SLABS)
        total = jnp.zeros((SLABS, SLABS), F32)
        for k in range(8):
            part = zt[pl.ds(k, SLABS, stride=8), :]
            total = total + part
            zhi[k * 128 : (k + 1) * 128, column], zlo[k * 128 : (k + 1) * 128, column] = split(part)
        under = lax.dot_general(
            lower, total, (((1,), (0,)), ((), ())),
            precision=lax.Precision.HIGHEST, preferred_element_type=F32,
        )
        zhi[1024:1152, column], zlo[1024:1152, column] = split(under)


def take_rows(frecv, rhi, rlo, stream, half):
    lane = lax.broadcasted_iota(jnp.int32, (SLABS, 128), 1)
    got = frecv[2 * stream + half]
    got = jnp.concatenate([got, jnp.zeros((SLABS, 96), F32)], axis=1)
    for i in range(4):
        tile, off = divmod(i * LINES, 128)
        lines = got[:, tile * 128 : tile * 128 + 128]
        if off:
            lines = pltpu.roll(lines, 128 - off, 1)
        if off + LINES > 128:
            more = got[:, tile * 128 + 128 : tile * 128 + 256]
            lines = jnp.where(lane < 128 - off, lines, pltpu.roll(more, 128 - off, 1))
        row = (4 * half + i) * SLABS
        rhi[stream, row : row + SLABS, :], rlo[stream, row : row + SLABS, :] = split(lines)


def pack(pieces):
    lane = lax.broadcasted_iota(jnp.int32, (SLABS, 128), 1)
    tiles = {}
    for at, block in pieces:
        tile, off = divmod(at, 128)
        moved = pltpu.roll(block, off, 1) if off else block
        tiles[tile] = jnp.where(lane >= off, moved, tiles[tile]) if off else moved
        if off + LINES > 128:
            tiles[tile + 1] = moved
    return tiles


def mix_lines(zhi, zlo, rhi, rlo, osend, below, stream):
    pieces = []
    for first in range(0, 9, 3):
        rows = slice(first * SLABS, (first + 3) * SLABS)
        mixed = dot3((zhi[rows, :], zlo[rows, :]), (rhi[stream], rlo[stream]))
        for k in range(3):
            pieces.append(((first + k) * LINES, mixed[k * SLABS : (k + 1) * SLABS]))
    if stream == 0:
        below[...] = pieces.pop()[1]
    else:
        pieces[8:] = [(8 * LINES, below[...]), (9 * LINES, pieces[8][1])]
    for tile, value in pack(pieces).items():
        last = min(tile * 128 + 128, osend.shape[1])
        osend[:, tile * 128 : last] = value[:, 0 : last - tile * 128]


def kernel(
    b, res, ymix, zmix, ret0, ret1,
    bp, ef, st, yv, zv, zt, zhi, zlo, rhi, rlo, fsend, frecv, osend0, osend1, below,
    fspare, spare0, spare1, hs, hr, send, recv, loads,
):
    gz, gx = lax.axis_index("gz"), lax.axis_index("gx")
    barrier = pltpu.get_barrier_semaphore()
    other = 1 - gx
    down, up = lax.rem(gz + SLABS - 1, SLABS), lax.rem(gz + 1, SLABS)

    def ready(peer):
        pl.semaphore_signal(barrier, inc=1, device_id={"gz": peer}, device_id_type=MESH)

    each_peer(gz, ready)
    bp[:, :, NX:XR, :] = jnp.zeros((4, 12, XR - NX, NY), F32)
    for z in (down, gz, up):
        pl.semaphore_signal(barrier, inc=1, device_id={"gz": z, "gx": other}, device_id_type=MESH)

    load_b = [pltpu.make_async_copy(b.at[:, :, z], bp.at[0:3, z + 2, 0:NX], loads.at[0]) for z in range(NZL)]
    load_r = [pltpu.make_async_copy(res.at[:, z], bp.at[3, z + 2, 0:NX], loads.at[1]) for z in range(NZL)]
    load_y = pltpu.make_async_copy(ymix, yv, loads.at[2])
    load_z = [pltpu.make_async_copy(zmix.at[:, k * 128 : (k + 1) * 128], zv.at[k], loads.at[3]) for k in range(8)]
    for copy in (*load_b, *load_r, load_y, *load_z):
        copy.start()
    load_y.wait()
    mixer = split(yv[...].T)
    pltpu.make_async_copy(bp.at[0:3, 2:10, 0:NX], bp.at[0:3, 2:10, 0:NX], loads.at[0]).wait()
    pltpu.make_async_copy(bp.at[3, 2:10, 0:NX], bp.at[3, 2:10, 0:NX], loads.at[1]).wait()
    pl.semaphore_wait(barrier, SLABS + 2)
    halo = halo_copies(bp, hs, hr)
    for copy in halo:
        copy.start()

    for copy in halo[:2]:
        copy.wait()

    @pl.loop(3, 9)
    def _(p):
        electric_plane(bp, ef, p)

    @pl.loop(2, 6)
    def _(r):
        stepped_plane(bp, ef, st, r)

    mix_rows(st[2 * LINES : 6 * LINES, :], mixer, fsend, 0)
    waits = [exchange(fsend.at[0], frecv.at[0], fspare.at[0], send.at[0], recv.at[0])]
    for copy in halo[2:]:
        copy.wait()

    @pl.when(gz == 0)
    def _():
        bp[:, 0:2] = jnp.zeros((4, 2, XR, NY), F32)

    @pl.when(gz == SLABS - 1)
    def _():
        bp[:, 10:12] = jnp.zeros((4, 2, XR, NY), F32)

    for p in (1, 2, 9, 10):
        electric_plane(bp, ef, p)
    for r in (0, 1, 6, 7):
        stepped_plane(bp, ef, st, r)
    edges = jnp.concatenate([st[6 * LINES :, :], st[0 : 2 * LINES, :]], axis=0)
    mix_rows(edges, mixer, fsend, 1)
    for block in range(1, 4):
        waits.append(exchange(fsend.at[block], frecv.at[block], fspare.at[block], send.at[block], recv.at[block]))
    pltpu.make_async_copy(zv, zv, loads.at[3]).wait()
    prepare(zv, zt, zhi, zlo, 0, NZL)

    for stream, (osend, back, spare) in enumerate(((osend0, ret0, spare0), (osend1, ret1, spare1))):
        for half in range(2):
            waits[2 * stream + half][0]()
            take_rows(frecv, rhi, rlo, stream, half)
        mix_lines(zhi, zlo, rhi, rlo, osend, below, stream)
        waits.append(exchange(osend, back, spare, send.at[4 + stream], recv.at[4 + stream]))
    for _, sent in waits[:4]:
        sent()
    for arrived, sent in waits[4:]:
        arrived()
        sent()


def finish(ret0, ret1, next_ref, pot_ref, r0, r1, tv, o1, o2, loads):
    load = [pltpu.make_async_copy(ret0, r0, loads.at[0]), pltpu.make_async_copy(ret1, r1, loads.at[1])]
    for copy in load:
        copy.start()
    for stream, (copy, got) in enumerate(zip(load, (r0, r1))):
        copy.wait()
        width = got.shape[1]
        for at in range(0, width, 128):
            last = min(at + 128, width)
            tv[stream, at:last, :] = got[:, at:last].T

    scale = float(NZL * SLABS) ** -0.5
    out = []
    for stream in range(2):
        column = tv[1, (8 + stream) * LINES : (9 + stream) * LINES, :]
        for k in range(NZL):
            lines = tv[stream, k * LINES : (k + 1) * LINES, :]
            column = column + lines
            o1[stream, pl.ds(k, LINES, stride=8), :] = lines
            for at, to, sign in ((0, 192, -1.0), (24, 0, 1.0), (48, 384, 1.0)):
                o2[stream, pl.ds(to + k, NX, stride=8), :] = column[at : at + NX] * (sign * scale)
        for i, (src, dst) in enumerate(((o1, next_ref), (o2, pot_ref))):
            lanes = slice(stream * 128, stream * 128 + 128)
            out.append(pltpu.make_async_copy(src.at[stream], dst.at[:, lanes], loads.at[2 + 2 * stream + i]))
            out[-1].start()
    for copy in out:
        copy.wait()


def on_device(b_field, resist, ymix, zmix):
    flat = (3 * NX * NZL, NY)
    dma = pltpu.SemaphoreType.DMA
    anywhere = pl.BlockSpec(memory_space=pl.ANY)
    widths = (8 * LINES, 10 * LINES)
    returned = pl.pallas_call(
        kernel,
        name="step",
        out_shape=tuple(jax.ShapeDtypeStruct((SLABS, width), F32) for width in widths),
        in_specs=[anywhere] * 4,
        out_specs=[anywhere] * 2,
        scratch_shapes=[
            pltpu.VMEM((4, NZL + 4, XR, NY), F32),
            pltpu.VMEM((3, NZL + 2, XR, NY), F32),
            pltpu.VMEM((LINES * NZL, NY), F32),
            pltpu.VMEM((NY, NY), F32),
            pltpu.VMEM((8, 1024, 128), F32),
            pltpu.VMEM((1024, 128), F32),
            pltpu.VMEM((1152, 1024), BF16),
            pltpu.VMEM((1152, 1024), BF16),
            pltpu.VMEM((2, 1024, 128), BF16),
            pltpu.VMEM((2, 1024, 128), BF16),
            pltpu.VMEM((4, SLABS, 4 * LINES), F32),
            pltpu.VMEM((4, SLABS, 4 * LINES), F32),
            pltpu.VMEM((SLABS, widths[0]), F32),
            pltpu.VMEM((SLABS, widths[1]), F32),
            pltpu.VMEM((SLABS, 128), F32),
            pltpu.VMEM((4, 8, 4 * LINES), F32),
            pltpu.VMEM((8, widths[0]), F32),
            pltpu.VMEM((8, widths[1]), F32),
            dma((8,)), dma((8,)), dma((6,)), dma((6,)), dma((4,)),
        ],
        compiler_params=pltpu.CompilerParams(
            collective_id=0, has_side_effects=True, vmem_limit_bytes=63 * 2**20
        ),
    )(b_field, resist, ymix, zmix)
    b_next, potential = pl.pallas_call(
        finish,
        name="finish",
        out_shape=(jax.ShapeDtypeStruct(flat, F32), jax.ShapeDtypeStruct(flat, F32)),
        in_specs=[anywhere] * 2,
        out_specs=[anywhere] * 2,
        scratch_shapes=[
            pltpu.VMEM((SLABS, widths[0]), F32),
            pltpu.VMEM((SLABS, widths[1]), F32),
            pltpu.VMEM((2, widths[1], 128), F32),
            pltpu.VMEM((2, flat[0], 128), F32),
            pltpu.VMEM((2, flat[0], 128), F32),
            dma((6,)),
        ],
        compiler_params=pltpu.CompilerParams(vmem_limit_bytes=63 * 2**20),
    )(*returned)
    return b_next.reshape(b_field.shape), potential.reshape(b_field.shape)


def solution(mesh):
    in_specs = (P(None, "gx", "gz", None), P("gx", "gz", None), P(), P())
    out_specs = (P(None, "gx", "gz", None), P(None, "gx", "gz", None))
    return jax.shard_map(
        on_device, mesh=mesh, in_specs=in_specs, out_specs=out_specs, check_vma=False
    )
```

```python
import functools

import jax
import jax.numpy as jnp
from jax import lax
from jax.experimental import pallas as pl
from jax.experimental.pallas import tpu as pltpu
from jax.sharding import PartitionSpec as P

MESH = pl.DeviceIdType.MESH
F32, BF16 = jnp.float32, jnp.bfloat16
TIME_STEP = 0.1
NX, NZL, NY = 24, 8, 256
LINES = 3 * NX
SLABS = 128
XR = 32


def split(value):
    high = value.astype(BF16)
    return high, (value - high.astype(F32)).astype(BF16)


def dot(lhs, rhs, rhs_dim=0):
    return lax.dot_general(
        lhs, rhs, (((1,), (rhs_dim,)), ((), ())), preferred_element_type=F32
    )


def dot3(lhs, rhs, rhs_dim=0):
    (lhs_hi, lhs_lo), (rhs_hi, rhs_lo) = lhs, rhs
    small = dot(lhs_lo, rhs_hi, rhs_dim) + dot(lhs_hi, rhs_lo, rhs_dim)
    return small + dot(lhs_hi, rhs_hi, rhs_dim)


def diff(value, axis):
    size = value.shape[axis]
    return pltpu.roll(value, size - 1, axis) - pltpu.roll(value, 1, axis)


def halo_copies(bp, send, recv):
    gz, gx = lax.axis_index("gz"), lax.axis_index("gx")
    down, up = lax.rem(gz + SLABS - 1, SLABS), lax.rem(gz + 1, SLABS)
    other = 1 - gx
    near, far = (NX - 1) * other, gx + (NX - 2) * other
    near_row, far_row = 24 + 7 * other, 25 + 5 * other
    rows = slice(0, NX)
    same, cross = lambda z: {"gz": z}, lambda z: {"gz": z, "gx": other}
    plan = (
        (bp.at[:, 2:10, near], bp.at[:, 2:10, near_row], cross(gz)),
        (bp.at[1:3, 2:10, far], bp.at[1:3, 2:10, far_row], cross(gz)),
        (bp.at[:, 2, rows], bp.at[:, 10, rows], same(down)),
        (bp.at[:, 9, rows], bp.at[:, 1, rows], same(up)),
        (bp.at[0:3, 2, near], bp.at[0:3, 10, near_row], cross(down)),
        (bp.at[0:3, 9, near], bp.at[0:3, 1, near_row], cross(up)),
        (bp.at[0:2, 3, rows], bp.at[0:2, 11, rows], same(down)),
        (bp.at[0:2, 8, rows], bp.at[0:2, 0, rows], same(up)),
    )
    return [
        pltpu.make_async_remote_copy(
            src_ref=src,
            dst_ref=dst,
            send_sem=send.at[i],
            recv_sem=recv.at[i],
            device_id=where,
            device_id_type=MESH,
        )
        for i, (src, dst, where) in enumerate(plan)
    ]


def each_peer(me, act):
    for offsets in ((4,), (3, 5), (2, 6), (1, 7)):

        @pl.loop(0, 16)
        def _(step):
            row = me + 8 * lax.rem(10 + 5 * step, 16)
            for z in offsets:
                act(lax.rem(row + z, SLABS))

    @pl.loop(1, 16)
    def _(step):
        act(lax.rem(me + 8 * step, SLABS))


def exchange(src, dst, spare, send, recv):
    me = lax.axis_index("gz")
    pltpu.make_async_copy(src.at[me], dst.at[me], recv).start()
    pltpu.make_async_copy(src.at[me], spare.at[0], send).start()

    def push(peer):
        pltpu.make_async_remote_copy(
            src_ref=src.at[peer],
            dst_ref=dst.at[me],
            send_sem=send,
            recv_sem=recv,
            device_id={"gz": peer},
            device_id_type=MESH,
        ).start()

    each_peer(me, push)

    def arrived():
        pltpu.make_async_copy(dst, dst, recv).wait()

    def sent():
        pltpu.make_async_copy(src, src, send).wait()

    return arrived, sent


def electric_plane(bp, ef, p):
    bx, by, bz, rs = bp[0, p], bp[1, p], bp[2, p], bp[3, p]
    jx = (diff(bz, 1) - (bp[1, p + 1] - bp[1, p - 1])) * 0.5
    jy = ((bp[0, p + 1] - bp[0, p - 1]) - diff(bz, 0)) * 0.5
    jz = (diff(by, 0) - diff(bx, 1)) * 0.5
    square = bx * bx + by * by + bz * bz
    inverse = 1.0 / (square + 1.0)
    along = (jx * bx + jy * by + jz * bz) * inverse
    factor = rs + square * inverse
    ef[0, p - 1] = jx * factor - bx * along
    ef[1, p - 1] = jy * factor - by * along
    ef[2, p - 1] = jz * factor - bz * along


def stepped_plane(bp, ef, st, r):
    ex, ey, ez = ef[0, r + 1], ef[1, r + 1], ef[2, r + 1]
    half = 0.5 * TIME_STEP
    cx = diff(ez, 1) - (ef[1, r + 2] - ef[1, r])
    cy = (ef[0, r + 2] - ef[0, r]) - diff(ez, 0)
    cz = diff(ey, 0) - diff(ex, 1)
    for c, curl in enumerate((cx, cy, cz)):
        row = pl.multiple_of(r * LINES + c * NX, 8)
        st[pl.ds(row, NX), :] = (bp[c, r + 2] - half * curl)[0:NX]


def mix_rows(rows, mixer, out, half):
    mixed = dot3(mixer, split(rows), 1)
    out[half] = mixed[0:SLABS]
    out[2 + half] = mixed[SLABS:]


def prepare(zv, zt, zhi, zlo, first, last):
    row_id = lax.broadcasted_iota(jnp.int32, (SLABS, SLABS), 0)
    col_id = lax.broadcasted_iota(jnp.int32, (SLABS, SLABS), 1)
    lower = (col_id < row_id).astype(F32)

    @pl.loop(first, last)
    def _(slot):
        r = lax.rem(slot + 2, NZL)
        for k in range(8):
            zt[k * 128 : (k + 1) * 128, :] = zv[k, pl.ds(r, SLABS, stride=8), :].T
        column = pl.ds(pl.multiple_of(slot * SLABS, SLABS), SLABS)
        total = jnp.zeros((SLABS, SLABS), F32)
        for k in range(8):
            part = zt[pl.ds(k, SLABS, stride=8), :]
            total = total + part
            zhi[k * 128 : (k + 1) * 128, column], zlo[k * 128 : (k + 1) * 128, column] = split(part)
        under = lax.dot_general(
            lower, total, (((1,), (0,)), ((), ())),
            precision=lax.Precision.HIGHEST, preferred_element_type=F32,
        )
        zhi[1024:1152, column], zlo[1024:1152, column] = split(under)


def take_rows(frecv, rhi, rlo, stream, half):
    lane = lax.broadcasted_iota(jnp.int32, (SLABS, 128), 1)
    got = frecv[2 * stream + half]
    got = jnp.concatenate([got, jnp.zeros((SLABS, 96), F32)], axis=1)
    for i in range(4):
        tile, off = divmod(i * LINES, 128)
        lines = got[:, tile * 128 : tile * 128 + 128]
        if off:
            lines = pltpu.roll(lines, 128 - off, 1)
        if off + LINES > 128:
            more = got[:, tile * 128 + 128 : tile * 128 + 256]
            lines = jnp.where(lane < 128 - off, lines, pltpu.roll(more, 128 - off, 1))
        row = (4 * half + i) * SLABS
        rhi[stream, row : row + SLABS, :], rlo[stream, row : row + SLABS, :] = split(lines)


def pack(pieces):
    lane = lax.broadcasted_iota(jnp.int32, (SLABS, 128), 1)
    tiles = {}
    for at, block in pieces:
        tile, off = divmod(at, 128)
        moved = pltpu.roll(block, off, 1) if off else block
        tiles[tile] = jnp.where(lane >= off, moved, tiles[tile]) if off else moved
        if off + LINES > 128:
            tiles[tile + 1] = moved
    return tiles


def mix_lines(zhi, zlo, rhi, rlo, osend, below, stream):
    pieces = []
    for first in range(0, 9, 3):
        rows = slice(first * SLABS, (first + 3) * SLABS)
        mixed = dot3((zhi[rows, :], zlo[rows, :]), (rhi[stream], rlo[stream]))
        for k in range(3):
            pieces.append(((first + k) * LINES, mixed[k * SLABS : (k + 1) * SLABS]))
    if stream == 0:
        below[...] = pieces.pop()[1]
    else:
        pieces[8:] = [(8 * LINES, below[...]), (9 * LINES, pieces[8][1])]
    for tile, value in pack(pieces).items():
        last = min(tile * 128 + 128, osend.shape[1])
        osend[:, tile * 128 : last] = value[:, 0 : last - tile * 128]


def kernel(
    b, res, ymix, zmix, ret0, ret1,
    bp, ef, st, yv, zv, zt, zhi, zlo, rhi, rlo, fsend, frecv, osend0, osend1, below,
    fspare, spare0, spare1, hs, hr, send, recv, loads,
):
    gz, gx = lax.axis_index("gz"), lax.axis_index("gx")
    load_b = [pltpu.make_async_copy(b.at[:, :, z], bp.at[0:3, z + 2, 0:NX], loads.at[0]) for z in range(NZL)]
    load_r = [pltpu.make_async_copy(res.at[:, z], bp.at[3, z + 2, 0:NX], loads.at[1]) for z in range(NZL)]
    for copy in (*load_b, *load_r):
        copy.start()
    barrier = pltpu.get_barrier_semaphore()
    other = 1 - gx
    down, up = lax.rem(gz + SLABS - 1, SLABS), lax.rem(gz + 1, SLABS)

    def ready(peer):
        pl.semaphore_signal(barrier, inc=1, device_id={"gz": peer}, device_id_type=MESH)

    each_peer(gz, ready)
    bp[:, :, NX:XR, :] = jnp.zeros((4, 12, XR - NX, NY), F32)
    for z in (down, gz, up):
        pl.semaphore_signal(barrier, inc=1, device_id={"gz": z, "gx": other}, device_id_type=MESH)

    load_y = pltpu.make_async_copy(ymix, yv, loads.at[2])
    load_z = [pltpu.make_async_copy(zmix.at[:, k * 128 : (k + 1) * 128], zv.at[k], loads.at[3]) for k in range(8)]
    for copy in (load_y, *load_z):
        copy.start()
    load_y.wait()
    mixer = split(yv[...].T)
    pltpu.make_async_copy(bp.at[0:3, 2:10, 0:NX], bp.at[0:3, 2:10, 0:NX], loads.at[0]).wait()
    pltpu.make_async_copy(bp.at[3, 2:10, 0:NX], bp.at[3, 2:10, 0:NX], loads.at[1]).wait()
    pl.semaphore_wait(barrier, SLABS + 2)
    halo = halo_copies(bp, hs, hr)
    for copy in halo:
        copy.start()

    for copy in halo[:2]:
        copy.wait()

    @pl.loop(3, 9)
    def _(p):
        electric_plane(bp, ef, p)

    @pl.loop(2, 6)
    def _(r):
        stepped_plane(bp, ef, st, r)

    mix_rows(st[2 * LINES : 6 * LINES, :], mixer, fsend, 0)
    waits = [exchange(fsend.at[0], frecv.at[0], fspare.at[0], send.at[0], recv.at[0])]
    for copy in halo[2:]:
        copy.wait()

    @pl.when(gz == 0)
    def _():
        bp[:, 0:2] = jnp.zeros((4, 2, XR, NY), F32)

    @pl.when(gz == SLABS - 1)
    def _():
        bp[:, 10:12] = jnp.zeros((4, 2, XR, NY), F32)

    for p in (1, 2, 9, 10):
        electric_plane(bp, ef, p)
    for r in (0, 1, 6, 7):
        stepped_plane(bp, ef, st, r)
    edges = jnp.concatenate([st[6 * LINES :, :], st[0 : 2 * LINES, :]], axis=0)
    mix_rows(edges, mixer, fsend, 1)
    for block in range(1, 4):
        waits.append(exchange(fsend.at[block], frecv.at[block], fspare.at[block], send.at[block], recv.at[block]))
    pltpu.make_async_copy(zv, zv, loads.at[3]).wait()
    prepare(zv, zt, zhi, zlo, 0, NZL)

    for stream, (osend, back, spare) in enumerate(((osend0, ret0, spare0), (osend1, ret1, spare1))):
        for half in range(2):
            waits[2 * stream + half][0]()
            take_rows(frecv, rhi, rlo, stream, half)
        mix_lines(zhi, zlo, rhi, rlo, osend, below, stream)
        waits.append(exchange(osend, back, spare, send.at[4 + stream], recv.at[4 + stream]))
    for _, sent in waits[:4]:
        sent()
    for arrived, sent in waits[4:]:
        arrived()
        sent()


def finish(ret0, ret1, next_ref, pot_ref, r0, r1, tv, o1, o2, loads):
    load = [pltpu.make_async_copy(ret0, r0, loads.at[0]), pltpu.make_async_copy(ret1, r1, loads.at[1])]
    for copy in load:
        copy.start()
    for stream, (copy, got) in enumerate(zip(load, (r0, r1))):
        copy.wait()
        width = got.shape[1]
        for at in range(0, width, 128):
            last = min(at + 128, width)
            tv[stream, at:last, :] = got[:, at:last].T

    scale = float(NZL * SLABS) ** -0.5
    out = []
    for stream in range(2):
        column = tv[1, (8 + stream) * LINES : (9 + stream) * LINES, :]
        for k in range(NZL):
            lines = tv[stream, k * LINES : (k + 1) * LINES, :]
            column = column + lines
            o1[stream, pl.ds(k, LINES, stride=8), :] = lines
            for at, to, sign in ((0, 192, -1.0), (24, 0, 1.0), (48, 384, 1.0)):
                o2[stream, pl.ds(to + k, NX, stride=8), :] = column[at : at + NX] * (sign * scale)
        for i, (src, dst) in enumerate(((o1, next_ref), (o2, pot_ref))):
            lanes = slice(stream * 128, stream * 128 + 128)
            out.append(pltpu.make_async_copy(src.at[stream], dst.at[:, lanes], loads.at[2 + 2 * stream + i]))
            out[-1].start()
    for copy in out:
        copy.wait()


def on_device(b_field, resist, ymix, zmix):
    flat = (3 * NX * NZL, NY)
    dma = pltpu.SemaphoreType.DMA
    anywhere = pl.BlockSpec(memory_space=pl.ANY)
    widths = (8 * LINES, 10 * LINES)
    returned = pl.pallas_call(
        kernel,
        name="step",
        out_shape=tuple(jax.ShapeDtypeStruct((SLABS, width), F32) for width in widths),
        in_specs=[anywhere] * 4,
        out_specs=[anywhere] * 2,
        scratch_shapes=[
            pltpu.VMEM((4, NZL + 4, XR, NY), F32),
            pltpu.VMEM((3, NZL + 2, XR, NY), F32),
            pltpu.VMEM((LINES * NZL, NY), F32),
            pltpu.VMEM((NY, NY), F32),
            pltpu.VMEM((8, 1024, 128), F32),
            pltpu.VMEM((1024, 128), F32),
            pltpu.VMEM((1152, 1024), BF16),
            pltpu.VMEM((1152, 1024), BF16),
            pltpu.VMEM((2, 1024, 128), BF16),
            pltpu.VMEM((2, 1024, 128), BF16),
            pltpu.VMEM((4, SLABS, 4 * LINES), F32),
            pltpu.VMEM((4, SLABS, 4 * LINES), F32),
            pltpu.VMEM((SLABS, widths[0]), F32),
            pltpu.VMEM((SLABS, widths[1]), F32),
            pltpu.VMEM((SLABS, 128), F32),
            pltpu.VMEM((4, 8, 4 * LINES), F32),
            pltpu.VMEM((8, widths[0]), F32),
            pltpu.VMEM((8, widths[1]), F32),
            dma((8,)), dma((8,)), dma((6,)), dma((6,)), dma((4,)),
        ],
        compiler_params=pltpu.CompilerParams(
            collective_id=0, has_side_effects=True, vmem_limit_bytes=63 * 2**20
        ),
    )(b_field, resist, ymix, zmix)
    b_next, potential = pl.pallas_call(
        finish,
        name="finish",
        out_shape=(jax.ShapeDtypeStruct(flat, F32), jax.ShapeDtypeStruct(flat, F32)),
        in_specs=[anywhere] * 2,
        out_specs=[anywhere] * 2,
        scratch_shapes=[
            pltpu.VMEM((SLABS, widths[0]), F32),
            pltpu.VMEM((SLABS, widths[1]), F32),
            pltpu.VMEM((2, widths[1], 128), F32),
            pltpu.VMEM((2, flat[0], 128), F32),
            pltpu.VMEM((2, flat[0], 128), F32),
            dma((6,)),
        ],
        compiler_params=pltpu.CompilerParams(vmem_limit_bytes=63 * 2**20),
    )(*returned)
    return b_next.reshape(b_field.shape), potential.reshape(b_field.shape)


def solution(mesh):
    in_specs = (P(None, "gx", "gz", None), P("gx", "gz", None), P(), P())
    out_specs = (P(None, "gx", "gz", None), P(None, "gx", "gz", None))
    return jax.shard_map(
        on_device, mesh=mesh, in_specs=in_specs, out_specs=out_specs, check_vma=False
    )
```

```python
import functools

import jax
import jax.numpy as jnp
from jax import lax
from jax.experimental import pallas as pl
from jax.experimental.pallas import tpu as pltpu
from jax.sharding import PartitionSpec as P

MESH = pl.DeviceIdType.MESH
F32, BF16 = jnp.float32, jnp.bfloat16
TIME_STEP = 0.1
NX, NZL, NY = 24, 8, 256
LINES = 3 * NX
SLABS = 128
XR = 32


def split(value):
    high = value.astype(BF16)
    return high, (value - high.astype(F32)).astype(BF16)


def dot(lhs, rhs, rhs_dim=0):
    return lax.dot_general(
        lhs, rhs, (((1,), (rhs_dim,)), ((), ())), preferred_element_type=F32
    )


def dot3(lhs, rhs, rhs_dim=0):
    (lhs_hi, lhs_lo), (rhs_hi, rhs_lo) = lhs, rhs
    small = dot(lhs_lo, rhs_hi, rhs_dim) + dot(lhs_hi, rhs_lo, rhs_dim)
    return small + dot(lhs_hi, rhs_hi, rhs_dim)


def diff(value, axis):
    size = value.shape[axis]
    return pltpu.roll(value, size - 1, axis) - pltpu.roll(value, 1, axis)


def halo_copies(bp, send, recv):
    gz, gx = lax.axis_index("gz"), lax.axis_index("gx")
    down, up = lax.rem(gz + SLABS - 1, SLABS), lax.rem(gz + 1, SLABS)
    other = 1 - gx
    near, far = (NX - 1) * other, gx + (NX - 2) * other
    near_row, far_row = 24 + 7 * other, 25 + 5 * other
    rows = slice(0, NX)
    same, cross = lambda z: {"gz": z}, lambda z: {"gz": z, "gx": other}
    plan = (
        (bp.at[:, 2:10, near], bp.at[:, 2:10, near_row], cross(gz)),
        (bp.at[1:3, 2:10, far], bp.at[1:3, 2:10, far_row], cross(gz)),
        (bp.at[:, 2, rows], bp.at[:, 10, rows], same(down)),
        (bp.at[:, 9, rows], bp.at[:, 1, rows], same(up)),
        (bp.at[0:3, 2, near], bp.at[0:3, 10, near_row], cross(down)),
        (bp.at[0:3, 9, near], bp.at[0:3, 1, near_row], cross(up)),
        (bp.at[0:2, 3, rows], bp.at[0:2, 11, rows], same(down)),
        (bp.at[0:2, 8, rows], bp.at[0:2, 0, rows], same(up)),
    )
    return [
        pltpu.make_async_remote_copy(
            src_ref=src,
            dst_ref=dst,
            send_sem=send.at[i],
            recv_sem=recv.at[i],
            device_id=where,
            device_id_type=MESH,
        )
        for i, (src, dst, where) in enumerate(plan)
    ]


def exchange(src, dst, spare, send, recv):
    me = lax.axis_index("gz")
    pltpu.make_async_copy(src.at[me], dst.at[me], recv).start()
    pltpu.make_async_copy(src.at[me], spare.at[0], send).start()

    @pl.loop(1, SLABS)
    def _(step):
        peer = lax.rem(me + step, SLABS)
        pltpu.make_async_remote_copy(
            src_ref=src.at[peer],
            dst_ref=dst.at[me],
            send_sem=send,
            recv_sem=recv,
            device_id={"gz": peer},
            device_id_type=MESH,
        ).start()

    def arrived():
        pltpu.make_async_copy(dst, dst, recv).wait()

    def sent():
        pltpu.make_async_copy(src, src, send).wait()

    return arrived, sent


def electric_plane(bp, ef, p):
    bx, by, bz, rs = bp[0, p], bp[1, p], bp[2, p], bp[3, p]
    jx = (diff(bz, 1) - (bp[1, p + 1] - bp[1, p - 1])) * 0.5
    jy = ((bp[0, p + 1] - bp[0, p - 1]) - diff(bz, 0)) * 0.5
    jz = (diff(by, 0) - diff(bx, 1)) * 0.5
    square = bx * bx + by * by + bz * bz
    inverse = 1.0 / (square + 1.0)
    along = (jx * bx + jy * by + jz * bz) * inverse
    factor = rs + square * inverse
    ef[0, p - 1] = jx * factor - bx * along
    ef[1, p - 1] = jy * factor - by * along
    ef[2, p - 1] = jz * factor - bz * along


def stepped_plane(bp, ef, st, r):
    ex, ey, ez = ef[0, r + 1], ef[1, r + 1], ef[2, r + 1]
    half = 0.5 * TIME_STEP
    cx = diff(ez, 1) - (ef[1, r + 2] - ef[1, r])
    cy = (ef[0, r + 2] - ef[0, r]) - diff(ez, 0)
    cz = diff(ey, 0) - diff(ex, 1)
    for c, curl in enumerate((cx, cy, cz)):
        row = pl.multiple_of(r * LINES + c * NX, 8)
        st[pl.ds(row, NX), :] = (bp[c, r + 2] - half * curl)[0:NX]


def mix_rows(rows, mixer, out, half):
    mixed = dot3(mixer, split(rows), 1)
    out[half] = mixed[0:SLABS]
    out[2 + half] = mixed[SLABS:]


def prepare(zv, zt, zhi, zlo, first, last):
    row_id = lax.broadcasted_iota(jnp.int32, (SLABS, SLABS), 0)
    col_id = lax.broadcasted_iota(jnp.int32, (SLABS, SLABS), 1)
    lower = (col_id < row_id).astype(F32)

    @pl.loop(first, last)
    def _(slot):
        r = lax.rem(slot + 2, NZL)
        for k in range(8):
            zt[k * 128 : (k + 1) * 128, :] = zv[k, pl.ds(r, SLABS, stride=8), :].T
        column = pl.ds(pl.multiple_of(slot * SLABS, SLABS), SLABS)
        total = jnp.zeros((SLABS, SLABS), F32)
        for k in range(8):
            part = zt[pl.ds(k, SLABS, stride=8), :]
            total = total + part
            zhi[k * 128 : (k + 1) * 128, column], zlo[k * 128 : (k + 1) * 128, column] = split(part)
        under = lax.dot_general(
            lower, total, (((1,), (0,)), ((), ())),
            precision=lax.Precision.HIGHEST, preferred_element_type=F32,
        )
        zhi[1024:1152, column], zlo[1024:1152, column] = split(under)


def take_rows(frecv, rhi, rlo, stream, half):
    lane = lax.broadcasted_iota(jnp.int32, (SLABS, 128), 1)
    got = frecv[2 * stream + half]
    got = jnp.concatenate([got, jnp.zeros((SLABS, 96), F32)], axis=1)
    for i in range(4):
        tile, off = divmod(i * LINES, 128)
        lines = got[:, tile * 128 : tile * 128 + 128]
        if off:
            lines = pltpu.roll(lines, 128 - off, 1)
        if off + LINES > 128:
            more = got[:, tile * 128 + 128 : tile * 128 + 256]
            lines = jnp.where(lane < 128 - off, lines, pltpu.roll(more, 128 - off, 1))
        row = (4 * half + i) * SLABS
        rhi[stream, row : row + SLABS, :], rlo[stream, row : row + SLABS, :] = split(lines)


def pack(pieces):
    lane = lax.broadcasted_iota(jnp.int32, (SLABS, 128), 1)
    tiles = {}
    for at, block in pieces:
        tile, off = divmod(at, 128)
        moved = pltpu.roll(block, off, 1) if off else block
        tiles[tile] = jnp.where(lane >= off, moved, tiles[tile]) if off else moved
        if off + LINES > 128:
            tiles[tile + 1] = moved
    return tiles


def mix_lines(zhi, zlo, rhi, rlo, osend, below, stream):
    pieces = []
    for first in range(0, 9, 3):
        rows = slice(first * SLABS, (first + 3) * SLABS)
        mixed = dot3((zhi[rows, :], zlo[rows, :]), (rhi[stream], rlo[stream]))
        for k in range(3):
            pieces.append(((first + k) * LINES, mixed[k * SLABS : (k + 1) * SLABS]))
    if stream == 0:
        below[...] = pieces.pop()[1]
    else:
        pieces[8:] = [(8 * LINES, below[...]), (9 * LINES, pieces[8][1])]
    for tile, value in pack(pieces).items():
        last = min(tile * 128 + 128, osend.shape[1])
        osend[:, tile * 128 : last] = value[:, 0 : last - tile * 128]


def kernel(
    b, res, ymix, zmix, ret0, ret1,
    bp, ef, st, yv, zv, zt, zhi, zlo, rhi, rlo, fsend, frecv, osend0, osend1, below,
    fspare, spare0, spare1, hs, hr, send, recv, loads,
):
    gz, gx = lax.axis_index("gz"), lax.axis_index("gx")
    load_b = [pltpu.make_async_copy(b.at[:, :, z], bp.at[0:3, z + 2, 0:NX], loads.at[0]) for z in range(NZL)]
    load_r = [pltpu.make_async_copy(res.at[:, z], bp.at[3, z + 2, 0:NX], loads.at[1]) for z in range(NZL)]
    load_y = pltpu.make_async_copy(ymix, yv, loads.at[2])
    load_z = [pltpu.make_async_copy(zmix.at[:, k * 128 : (k + 1) * 128], zv.at[k], loads.at[3]) for k in range(8)]
    for copy in (*load_b, *load_r, load_y, *load_z):
        copy.start()
    bp[:, :, NX:XR, :] = jnp.zeros((4, 12, XR - NX, NY), F32)

    barrier = pltpu.get_barrier_semaphore()
    other = 1 - gx
    down, up = lax.rem(gz + SLABS - 1, SLABS), lax.rem(gz + 1, SLABS)
    for z in (down, gz, up):
        pl.semaphore_signal(barrier, inc=1, device_id={"gz": z, "gx": other}, device_id_type=MESH)

    @pl.loop(1, SLABS)
    def _(step):
        peer = lax.rem(gz + step, SLABS)
        pl.semaphore_signal(barrier, inc=1, device_id={"gz": peer}, device_id_type=MESH)

    load_y.wait()
    mixer = split(yv[...].T)
    pltpu.make_async_copy(bp.at[0:3, 2:10, 0:NX], bp.at[0:3, 2:10, 0:NX], loads.at[0]).wait()
    pltpu.make_async_copy(bp.at[3, 2:10, 0:NX], bp.at[3, 2:10, 0:NX], loads.at[1]).wait()
    pl.semaphore_wait(barrier, SLABS + 2)
    halo = halo_copies(bp, hs, hr)
    for copy in halo:
        copy.start()

    for copy in halo[:2]:
        copy.wait()

    @pl.loop(3, 9)
    def _(p):
        electric_plane(bp, ef, p)

    @pl.loop(2, 6)
    def _(r):
        stepped_plane(bp, ef, st, r)

    mix_rows(st[2 * LINES : 6 * LINES, :], mixer, fsend, 0)
    waits = [exchange(fsend.at[0], frecv.at[0], fspare.at[0], send.at[0], recv.at[0])]
    for copy in halo[2:]:
        copy.wait()

    @pl.when(gz == 0)
    def _():
        bp[:, 0:2] = jnp.zeros((4, 2, XR, NY), F32)

    @pl.when(gz == SLABS - 1)
    def _():
        bp[:, 10:12] = jnp.zeros((4, 2, XR, NY), F32)

    for p in (1, 2, 9, 10):
        electric_plane(bp, ef, p)
    for r in (0, 1, 6, 7):
        stepped_plane(bp, ef, st, r)
    edges = jnp.concatenate([st[6 * LINES :, :], st[0 : 2 * LINES, :]], axis=0)
    mix_rows(edges, mixer, fsend, 1)
    for block in range(1, 4):
        waits.append(exchange(fsend.at[block], frecv.at[block], fspare.at[block], send.at[block], recv.at[block]))
    pltpu.make_async_copy(zv, zv, loads.at[3]).wait()
    prepare(zv, zt, zhi, zlo, 0, NZL)

    for stream, (osend, back, spare) in enumerate(((osend0, ret0, spare0), (osend1, ret1, spare1))):
        for half in range(2):
            waits[2 * stream + half][0]()
            take_rows(frecv, rhi, rlo, stream, half)
        mix_lines(zhi, zlo, rhi, rlo, osend, below, stream)
        waits.append(exchange(osend, back, spare, send.at[4 + stream], recv.at[4 + stream]))
    for _, sent in waits[:4]:
        sent()
    for arrived, sent in waits[4:]:
        arrived()
        sent()


def finish(ret0, ret1, next_ref, pot_ref, r0, r1, tv, o1, o2, loads):
    load = [pltpu.make_async_copy(ret0, r0, loads.at[0]), pltpu.make_async_copy(ret1, r1, loads.at[1])]
    for copy in load:
        copy.start()
    for stream, (copy, got) in enumerate(zip(load, (r0, r1))):
        copy.wait()
        width = got.shape[1]
        for at in range(0, width, 128):
            last = min(at + 128, width)
            tv[stream, at:last, :] = got[:, at:last].T

    scale = float(NZL * SLABS) ** -0.5
    out = []
    for stream in range(2):
        column = tv[1, (8 + stream) * LINES : (9 + stream) * LINES, :]
        for k in range(NZL):
            lines = tv[stream, k * LINES : (k + 1) * LINES, :]
            column = column + lines
            o1[stream, pl.ds(k, LINES, stride=8), :] = lines
            for at, to, sign in ((0, 192, -1.0), (24, 0, 1.0), (48, 384, 1.0)):
                o2[stream, pl.ds(to + k, NX, stride=8), :] = column[at : at + NX] * (sign * scale)
        for i, (src, dst) in enumerate(((o1, next_ref), (o2, pot_ref))):
            lanes = slice(stream * 128, stream * 128 + 128)
            out.append(pltpu.make_async_copy(src.at[stream], dst.at[:, lanes], loads.at[2 + 2 * stream + i]))
            out[-1].start()
    for copy in out:
        copy.wait()


def on_device(b_field, resist, ymix, zmix):
    flat = (3 * NX * NZL, NY)
    dma = pltpu.SemaphoreType.DMA
    anywhere = pl.BlockSpec(memory_space=pl.ANY)
    widths = (8 * LINES, 10 * LINES)
    returned = pl.pallas_call(
        kernel,
        name="step",
        out_shape=tuple(jax.ShapeDtypeStruct((SLABS, width), F32) for width in widths),
        in_specs=[anywhere] * 4,
        out_specs=[anywhere] * 2,
        scratch_shapes=[
            pltpu.VMEM((4, NZL + 4, XR, NY), F32),
            pltpu.VMEM((3, NZL + 2, XR, NY), F32),
            pltpu.VMEM((LINES * NZL, NY), F32),
            pltpu.VMEM((NY, NY), F32),
            pltpu.VMEM((8, 1024, 128), F32),
            pltpu.VMEM((1024, 128), F32),
            pltpu.VMEM((1152, 1024), BF16),
            pltpu.VMEM((1152, 1024), BF16),
            pltpu.VMEM((2, 1024, 128), BF16),
            pltpu.VMEM((2, 1024, 128), BF16),
            pltpu.VMEM((4, SLABS, 4 * LINES), F32),
            pltpu.VMEM((4, SLABS, 4 * LINES), F32),
            pltpu.VMEM((SLABS, widths[0]), F32),
            pltpu.VMEM((SLABS, widths[1]), F32),
            pltpu.VMEM((SLABS, 128), F32),
            pltpu.VMEM((4, 8, 4 * LINES), F32),
            pltpu.VMEM((8, widths[0]), F32),
            pltpu.VMEM((8, widths[1]), F32),
            dma((8,)), dma((8,)), dma((6,)), dma((6,)), dma((4,)),
        ],
        compiler_params=pltpu.CompilerParams(
            collective_id=0, has_side_effects=True, vmem_limit_bytes=63 * 2**20
        ),
    )(b_field, resist, ymix, zmix)
    b_next, potential = pl.pallas_call(
        finish,
        name="finish",
        out_shape=(jax.ShapeDtypeStruct(flat, F32), jax.ShapeDtypeStruct(flat, F32)),
        in_specs=[anywhere] * 2,
        out_specs=[anywhere] * 2,
        scratch_shapes=[
            pltpu.VMEM((SLABS, widths[0]), F32),
            pltpu.VMEM((SLABS, widths[1]), F32),
            pltpu.VMEM((2, widths[1], 128), F32),
            pltpu.VMEM((2, flat[0], 128), F32),
            pltpu.VMEM((2, flat[0], 128), F32),
            dma((6,)),
        ],
        compiler_params=pltpu.CompilerParams(vmem_limit_bytes=63 * 2**20),
    )(*returned)
    return b_next.reshape(b_field.shape), potential.reshape(b_field.shape)


def solution(mesh):
    in_specs = (P(None, "gx", "gz", None), P("gx", "gz", None), P(), P())
    out_specs = (P(None, "gx", "gz", None), P(None, "gx", "gz", None))
    return jax.shard_map(
        on_device, mesh=mesh, in_specs=in_specs, out_specs=out_specs, check_vma=False
    )
```
